32 devices in a mesh: ctx: 8 (over z, x), ch: 4 (over y, core).
Axes of the slice: x: 2, y: 2, z: 4, core: 2. Of those that a mesh axis runs over, the one named last changes fastest.
Arguments:
- query_input: bfloat16 [4096, 4096], P('ch', 'ctx'), may hold values from -6 to 6
- key_input: bfloat16 [4096, 4096], P('ch', 'ctx'), may hold values from -6 to 6
- value_input: bfloat16 [4096, 4096], P('ch', 'ctx'), may hold values from -6 to 6
- decay_rate: float32 [8, 16], P('ch'), may hold values from 0 to 1, as said below
- residue: float32 [8, 16], P('ch'), may hold values from -1 to 1
- doc_ends: int32 [4], replicated, may hold values from 1 to 4096, as said below
- out_weight: bfloat16 [4096, 4096], P(None, 'ch'), may hold values from -0.09375 to 0.09375
- out_cotangent: bfloat16 [4096, 4096], P('ctx', 'ch'), may hold values from -6 to 6
Outputs:
- query_grad: bfloat16 [4096, 4096], P('ch', 'ctx')
- key_grad: bfloat16 [4096, 4096], P('ch', 'ctx')
- value_grad: bfloat16 [4096, 4096], P('ch', 'ctx')
- weight_grad: float32 [4096, 4096], P('ctx', 'ch')
The draws below stay inside these ranges and needn't reach their ends.
Inputs may be any that keep to these rules, and one draw needn't show every extreme that they name: `doc_ends`: strictly increasing; the last entry equals 4096. `decay_rate`: positive.
All inputs are finite; a program needn't handle non-finite values.
Results may differ from the reference program's by a relative error of at most 0.0029.
Values may be sent and summed in bfloat16 or wider, within the bound.
A program may use at most 128 MiB of HBM per device.

```python
import math
from functools import partial
import jax
import jax.numpy as jnp
from jax import lax

D = 4096
GROUP_CH = 512
POLES = 16
TOK_DEV = 512
DOCS = 4
FILTERS = 8
CHANNELS = 4096
SEQ = 4096
N_CTX = 8


def filter_poles(key):
    base = jax.random.fold_in(key, 11)
    pick_key, slow_key, fast_key, sign_key = jax.random.split(base, 4)
    pole_shape = (FILTERS, POLES)
    slow_share = 0.5
    slow_pick = jax.random.uniform(pick_key, pole_shape, jnp.float32) < slow_share
    slow_decays = math.log(10.0) / SEQ * jnp.exp(jax.random.uniform(slow_key, pole_shape, jnp.float32, math.log(0.05), 0.0))
    fast_decays = jax.random.uniform(fast_key, pole_shape, jnp.float32, 1.0 / 50.0, 1.0 / 30.0)
    decays = jnp.where(slow_pick, slow_decays, fast_decays)
    amplitudes = jnp.clip(jax.random.normal(sign_key, pole_shape, jnp.float32), -4.0, 4.0) * jnp.sqrt(2.0 * decays) * 0.5
    return (decays, amplitudes)


def draw_decay_rate(key, part):
    return filter_poles(key)[0].astype(jnp.float32)


def draw_residue(key, part):
    return filter_poles(key)[1].astype(jnp.float32)


def draw_doc_ends(key, part):
    picks = jax.random.permutation(jax.random.fold_in(key, 23), SEQ - 1)[:DOCS - 1] + 1
    inner = jnp.sort(picks.astype(jnp.int32))
    return jnp.concatenate([inner, jnp.full((1,), SEQ, jnp.int32)]).astype(jnp.int32)


def shard_levels(stream_key, extent, shards, smallest, largest):
    def one(dim, shards_of):
        heights = jax.random.uniform(jax.random.fold_in(jax.random.fold_in(stream_key, 6), dim), (shards_of,), jnp.float32, smallest / len(shards), largest / len(shards))
        return jnp.repeat(jnp.exp(heights), extent[dim] // shards_of).reshape((-1,) + (1,) * (len(extent) - dim - 1))

    factor_of = one(*shards[0])
    for cut in shards[1:]:
        factor_of = factor_of * one(*cut)
    return factor_of


def centred(stream_key, extent, deviation, bound, cuts=(), kind=jnp.bfloat16):
    values = jax.random.normal(stream_key, extent, jnp.float32) * deviation
    if len(cuts) > 0:
        values = shard_levels(stream_key, extent, cuts, -0.22, 0.18) * values
    return jnp.clip(values, min=-bound, max=bound).astype(kind)


def setup_inputs(seed: int = 0) -> dict:
    keys = jax.random.split(jax.random.key(seed), 9)
    return {
        "query_input": centred(keys[0], (CHANNELS, SEQ), 1.0, 6.0, ((0, 4), (1, 8))),
        "key_input": centred(keys[1], (CHANNELS, SEQ), 1.0, 6.0, ((0, 4), (1, 8))),
        "value_input": centred(keys[2], (CHANNELS, SEQ), 1.0, 6.0, ((0, 4), (1, 8))),
        "decay_rate": draw_decay_rate(jax.random.fold_in(keys[8], 71), 0),
        "residue": draw_residue(jax.random.fold_in(keys[8], 71), 0),
        "doc_ends": draw_doc_ends(jax.random.fold_in(keys[8], 71), 0),
        "out_weight": centred(keys[6], (CHANNELS, D), CHANNELS ** -0.5, 0.09375, ((1, 4),)),
        "out_cotangent": centred(keys[7], (SEQ, D), 1.0, 6.0, ((0, 8), (1, 4))),
    }


def block_maps(block_index, doc_ids, decays, weights):
    anchor = (block_index * TOK_DEV).astype(jnp.int32)
    offsets = jnp.arange(TOK_DEV, dtype=jnp.int32)
    ids = lax.dynamic_slice_in_dim(doc_ids, anchor, TOK_DEV)
    previous = jnp.where(block_index > 0, doc_ids[jnp.maximum(anchor - 1, 0).astype(jnp.int32)], -1)
    place = offsets.astype(jnp.float32)
    lags = place[:, None] - place[None, :]
    causal = (lags >= 0.0) & (ids[:, None] == ids[None, :])
    powers = jnp.exp(-decays[:, None, None] * jnp.maximum(lags, 0.0)[None, :, :])
    kernel = jnp.einsum('n,nts->ts', weights, powers, precision=lax.Precision.HIGHEST)
    kernel = jnp.where(causal, kernel, 0.0)
    alive_mask = (ids == previous).astype(jnp.float32)
    tail_mask = (ids == ids[-1]).astype(jnp.float32)
    carry_in_map = weights[:, None] * jnp.exp(-decays[:, None] * (place + 1.0)[None, :]) * alive_mask[None, :]
    carry_out_map = jnp.exp(-decays[:, None] * (TOK_DEV - 1.0 - place)[None, :]) * tail_mask[None, :]
    back_out_map = jnp.exp(-decays[:, None] * place[None, :]) * alive_mask[None, :]
    back_in_map = weights[:, None] * jnp.exp(-decays[:, None] * (TOK_DEV - place)[None, :]) * tail_mask[None, :]
    transit = jnp.exp(-decays * TOK_DEV) * (ids[-1] == previous).astype(jnp.float32)
    return (kernel, carry_in_map, carry_out_map, back_out_map, back_in_map, transit)

def group_pass(doc_ids, operands):
    mixed, signal, decays, weights = operands
    group_ch = mixed.shape[0]
    mixed_blocks = mixed.reshape(group_ch, N_CTX, TOK_DEV).transpose(1, 0, 2)
    signal_blocks = signal.reshape(group_ch, N_CTX, TOK_DEV).transpose(1, 0, 2)
    block_ids = jnp.arange(N_CTX, dtype=jnp.int32)
    start_state = jnp.zeros((POLES, group_ch), jnp.float32)

    def forward_step(state, inputs):
        block_index, block_in = inputs
        kernel, carry_in_map, carry_out_map, back_out_map, back_in_map, transit = block_maps(block_index, doc_ids, decays, weights)
        result = jnp.dot(block_in, kernel.T, precision=lax.Precision.HIGHEST)
        result = result + jnp.dot(state.T, carry_in_map, precision=lax.Precision.HIGHEST)
        state = transit[:, None] * state + jnp.dot(carry_out_map, block_in.T, precision=lax.Precision.HIGHEST)
        return (state, result)

    def backward_step(state, inputs):
        block_index, block_grad = inputs
        kernel, carry_in_map, carry_out_map, back_out_map, back_in_map, transit = block_maps(block_index, doc_ids, decays, weights)
        result = jnp.dot(block_grad, kernel, precision=lax.Precision.HIGHEST)
        result = result + jnp.dot(state.T, back_in_map, precision=lax.Precision.HIGHEST)
        state = transit[:, None] * state + jnp.dot(back_out_map, block_grad.T, precision=lax.Precision.HIGHEST)
        return (state, result)
    final_fwd, filtered = lax.scan(forward_step, start_state, (block_ids, mixed_blocks))
    final_bwd, spread = lax.scan(backward_step, start_state, (block_ids, signal_blocks), reverse=True)
    filtered = filtered.transpose(1, 0, 2).reshape(group_ch, SEQ)
    spread = spread.transpose(1, 0, 2).reshape(group_ch, SEQ)
    return (filtered, spread)

def reference(query_input, key_input, value_input, decay_rate, residue, doc_ends, out_weight, out_cotangent):
    positions = jnp.arange(SEQ, dtype=jnp.int32)
    doc_ids = lax.optimization_barrier(jnp.sum((doc_ends[None, :] <= positions[:, None]).astype(jnp.int32), axis=1)).astype(jnp.int32)
    output_grad = jnp.dot(out_weight, out_cotangent.T, preferred_element_type=jnp.float32)
    query_f = query_input.astype(jnp.float32)
    key_f = key_input.astype(jnp.float32)
    value_f = value_input.astype(jnp.float32)
    mixed = key_f * value_f
    signal = output_grad * query_f
    mixed_groups = mixed.reshape(FILTERS, GROUP_CH, SEQ)
    signal_groups = signal.reshape(FILTERS, GROUP_CH, SEQ)
    filtered, spread = lax.map(partial(group_pass, doc_ids), (mixed_groups, signal_groups, decay_rate, residue))
    filtered = filtered.reshape(CHANNELS, SEQ)
    spread = spread.reshape(CHANNELS, SEQ)
    gated = (query_f * filtered).astype(jnp.bfloat16)
    query_grad = (output_grad * filtered).astype(jnp.bfloat16)
    key_grad = (spread * value_f).astype(jnp.bfloat16)
    value_grad = (spread * key_f).astype(jnp.bfloat16)
    weight_grad = jnp.dot(gated, out_cotangent, preferred_element_type=jnp.float32) * (1.0 / math.sqrt(SEQ))
    return (query_grad, key_grad, value_grad, weight_grad)
```

```python
import math

import jax
import jax.numpy as jnp
from jax import lax
from jax.sharding import PartitionSpec as P

HIGH = lax.Precision.HIGH
TILE = 128


def doc_of(doc_ends, positions):
    return jnp.sum((doc_ends[None, :] <= positions[:, None]).astype(jnp.int32), axis=1)


def local_kernel(decay_rate, residue, doc_ids, length):
    groups = decay_rate.shape[0]
    place = jnp.arange(length, dtype=jnp.float32)
    narrow = jnp.arange(TILE, dtype=jnp.float32)
    half = 0.5 * TILE
    rising = jnp.exp(-decay_rate[:, None, :] * (place - half)[None, :, None]) * residue[:, None, :]
    falling = jnp.exp(decay_rate[:, None, :] * (narrow - half)[None, :, None])
    strip = jnp.einsum("gtn,gsn->gts", rising, falling, precision=lax.Precision.HIGHEST)
    columns = []
    for start in range(0, length, TILE):
        top = jnp.zeros((groups, start, TILE), jnp.float32)
        columns.append(jnp.concatenate([top, strip[:, : length - start]], axis=1))
    kernel = jnp.concatenate(columns, axis=2)
    offsets = jnp.arange(length, dtype=jnp.int32)
    causal = (offsets[:, None] >= offsets[None, :]) & (doc_ids[:, None] == doc_ids[None, :])
    return jnp.where(causal[None], kernel, 0.0)


def exchange_rows(gated, n_ctx, n_ch):
    rows, length = gated.shape
    mine = rows * n_ch // n_ctx
    pieces = gated.reshape(n_ctx // n_ch, n_ch, mine // n_ch, length)
    pieces = lax.all_to_all(pieces, "ch", split_axis=1, concat_axis=0, tiled=True)
    pieces = pieces.reshape(n_ctx, mine // n_ch, length)
    pieces = lax.all_to_all(pieces, "ctx", split_axis=0, concat_axis=0, tiled=True)
    pieces = pieces.transpose(1, 0, 2).reshape(mine // n_ch, n_ctx * length)
    return lax.all_gather(pieces, "ch", axis=0, tiled=True)


def local(
    query_input, key_input, value_input, decay_rate, residue, doc_ends, out_weight, out_cotangent
):
    rows_here, length = query_input.shape
    n_ctx, n_ch = lax.axis_size("ctx"), lax.axis_size("ch")
    groups = decay_rate.shape[0]
    group_rows = rows_here // groups
    me = lax.axis_index("ctx")
    offsets = jnp.arange(length, dtype=jnp.int32)
    place = offsets.astype(jnp.float32)
    doc_ids = doc_of(doc_ends, me * length + offsets)
    blocks = jnp.arange(n_ctx, dtype=jnp.int32)
    last_ids = doc_of(doc_ends, (blocks + 1) * length - 1)
    previous = jnp.where(me > 0, jnp.sum((doc_ends <= me * length - 1).astype(jnp.int32)), -1)
    last = doc_ids[-1]

    cotangent_all = lax.all_gather(out_cotangent, "ctx", axis=0, tiled=True)

    alive_mask = (doc_ids == previous).astype(jnp.float32)
    tail_mask = (doc_ids == last).astype(jnp.float32)
    rate = decay_rate[:, :, None]
    carry_in_map = residue[:, :, None] * jnp.exp(-rate * (place + 1.0)) * alive_mask
    carry_out_map = jnp.exp(-rate * (length - 1.0 - place)) * tail_mask
    back_out_map = jnp.exp(-rate * place) * alive_mask
    back_in_map = residue[:, :, None] * jnp.exp(-rate * (length - place)) * tail_mask
    steps_ahead = me - 1 - blocks
    joined_ahead = (steps_ahead >= 0) & (last_ids == previous)
    ahead_weight = jnp.where(
        joined_ahead[:, None, None],
        jnp.exp(-decay_rate[None] * (length * jnp.maximum(steps_ahead, 0)).astype(jnp.float32)[:, None, None]),
        0.0,
    )
    steps_back = blocks - 1 - me
    before_ids = jnp.concatenate([jnp.full((1,), -1, jnp.int32), last_ids[:-1]])
    joined_back = (steps_back >= 0) & (before_ids == last)
    back_weight = jnp.where(
        joined_back[:, None, None],
        jnp.exp(-decay_rate[None] * (length * jnp.maximum(steps_back, 0)).astype(jnp.float32)[:, None, None]),
        0.0,
    )

    key_f = key_input.astype(jnp.float32)
    value_f = value_input.astype(jnp.float32)
    query_f = query_input.astype(jnp.float32)
    mixed = (key_f * value_f).reshape(groups, group_rows, length)
    forward_part = jnp.einsum("gnl,gcl->gnc", carry_out_map, mixed, precision=HIGH)
    forward_all = lax.all_gather(forward_part, "ctx", axis=0)
    entering = jnp.sum(ahead_weight[..., None] * forward_all, axis=0)

    partial_grad = lax.dot_general(
        out_weight, out_cotangent, (((1,), (1,)), ((), ())), preferred_element_type=jnp.float32
    )
    output_grad = lax.psum_scatter(partial_grad, "ch", scatter_dimension=0, tiled=True)

    kernel = local_kernel(decay_rate, residue, doc_ids, length)
    filtered = jnp.einsum("gcs,gts->gct", mixed, kernel, precision=HIGH)
    filtered = filtered + jnp.einsum("gnc,gnt->gct", entering, carry_in_map, precision=HIGH)
    filtered = filtered.reshape(rows_here, length)
    gated = (query_f * filtered).astype(jnp.bfloat16)
    gated_rows = exchange_rows(gated, n_ctx, n_ch)

    signal = (output_grad * query_f).reshape(groups, group_rows, length)
    backward_part = jnp.einsum("gnl,gcl->gnc", back_out_map, signal, precision=HIGH)
    backward_all = lax.all_gather(backward_part, "ctx", axis=0)
    query_grad = (output_grad * filtered).astype(jnp.bfloat16)
    spread = jnp.einsum("gct,gts->gcs", signal, kernel, precision=HIGH)
    returning = jnp.sum(back_weight[..., None] * backward_all, axis=0)
    spread = spread + jnp.einsum("gnc,gns->gcs", returning, back_in_map, precision=HIGH)
    spread = spread.reshape(rows_here, length)
    key_grad = (spread * value_f).astype(jnp.bfloat16)
    value_grad = (spread * key_f).astype(jnp.bfloat16)

    norm_factor = 1.0 / math.sqrt(length * n_ctx)
    weight_grad = jnp.dot(gated_rows, cotangent_all, preferred_element_type=jnp.float32) * norm_factor
    return (query_grad, key_grad, value_grad, weight_grad)


def solution(mesh):
    return jax.shard_map(
        local,
        mesh=mesh,
        in_specs=(
            P("ch", "ctx"),
            P("ch", "ctx"),
            P("ch", "ctx"),
            P("ch", None),
            P("ch", None),
            P(),
            P(None, "ch"),
            P("ctx", "ch"),
        ),
        out_specs=(P("ch", "ctx"), P("ch", "ctx"), P("ch", "ctx"), P("ctx", "ch")),
        check_vma=False,
    )
```

```python
import functools
import math

import jax
import jax.numpy as jnp
from jax import lax
from jax.experimental import pallas as pl
from jax.experimental.pallas import tpu as pltpu
from jax.sharding import PartitionSpec as P

MESH = pl.DeviceIdType.MESH
HIGH = lax.Precision.HIGH
TILE = 128
CUT = 96


def doc_of(doc_ends, positions):
    return jnp.sum((doc_ends[None, :] <= positions[:, None]).astype(jnp.int32), axis=1)


def local_kernel(decay_rate, residue, doc_ids, length):
    groups = decay_rate.shape[0]
    place = jnp.arange(length, dtype=jnp.float32)
    narrow = jnp.arange(TILE, dtype=jnp.float32)
    half = 0.5 * TILE
    rising = jnp.exp(-decay_rate[:, None, :] * (place - half)[None, :, None]) * residue[:, None, :]
    falling = jnp.exp(decay_rate[:, None, :] * (narrow - half)[None, :, None])
    strip = jnp.einsum("gtn,gsn->gts", rising, falling, precision=lax.Precision.HIGHEST)
    columns = []
    for start in range(0, length, TILE):
        top = jnp.zeros((groups, start, TILE), jnp.float32)
        columns.append(jnp.concatenate([top, strip[:, : length - start]], axis=1))
    kernel = jnp.concatenate(columns, axis=2)
    offsets = jnp.arange(length, dtype=jnp.int32)
    causal = (offsets[:, None] >= offsets[None, :]) & (doc_ids[:, None] == doc_ids[None, :])
    return jnp.where(causal[None], kernel, 0.0)


def exchange_rows(gated, n_ctx, n_ch):
    rows, length = gated.shape
    mine = rows * n_ch // n_ctx
    pieces = gated.reshape(n_ctx // n_ch, n_ch, mine // n_ch, length)
    pieces = lax.all_to_all(pieces, "ch", split_axis=1, concat_axis=0, tiled=True)
    pieces = pieces.reshape(n_ctx, mine // n_ch, length)
    pieces = lax.all_to_all(pieces, "ctx", split_axis=0, concat_axis=0, tiled=True)
    pieces = pieces.transpose(1, 0, 2).reshape(mine // n_ch, n_ctx * length)
    return lax.all_gather(pieces, "ch", axis=0, tiled=True)


def ctx_id(index):
    return (index, lax.axis_index("ch"))


def ch_id(index):
    return (lax.axis_index("ctx"), index)


def remote(src, dst, send, recv, device):
    return pltpu.make_async_remote_copy(
        src_ref=src, dst_ref=dst, send_sem=send, recv_sem=recv, device_id=device, device_id_type=MESH
    )


def greet(devices):
    barrier = pltpu.get_barrier_semaphore()
    for device in devices:
        pl.semaphore_signal(barrier, inc=1, device_id=device, device_id_type=MESH)
    pl.semaphore_wait(barrier, len(devices))


def state_kernel(n_ctx, sign, part_ref, all_ref, send, recv):
    me = lax.axis_index("ctx")
    greet([ctx_id(lax.rem(me + d, n_ctx)) for d in range(1, n_ctx)])

    def inside(index):
        return (index >= 0) & (index < n_ctx)

    for d in range(1, n_ctx):
        to = me + sign * d

        @pl.when(inside(to))
        def _():
            remote(part_ref, all_ref.at[me], send.at[d], recv.at[d], ctx_id(to)).start()

    for d in range(1, n_ctx):
        to, came = me + sign * d, me - sign * d

        @pl.when(inside(came))
        def _():
            remote(part_ref, all_ref.at[came], send.at[d], recv.at[d], ctx_id(came)).wait_recv()

        @pl.when(inside(to))
        def _():
            remote(part_ref, all_ref.at[me], send.at[d], recv.at[d], ctx_id(to)).wait_send()


def spread_states(part, sign, number):
    n_ctx = lax.axis_size("ctx")
    if n_ctx != 8:
        return lax.all_gather(part, "ctx", axis=0)
    any_space = pl.BlockSpec(memory_space=pl.ANY)
    return pl.pallas_call(
        functools.partial(state_kernel, n_ctx, sign),
        out_shape=jax.ShapeDtypeStruct((n_ctx,) + part.shape, part.dtype),
        in_specs=[any_space],
        out_specs=any_space,
        scratch_shapes=[pltpu.SemaphoreType.DMA((n_ctx,)), pltpu.SemaphoreType.DMA((n_ctx,))],
        compiler_params=pltpu.CompilerParams(collective_id=number, has_side_effects=True),
        name="states_ahead" if sign > 0 else "states_back",
    )(part)


def move_kernel(
    cut, cot_ref, gated_ref, cots_ref, rows_ref, turned_ref, joined_ref,
    own_sem, f_recv, g_recv, q_recv, f_send, g_send, p_send, q_send,
    turn_send, turn_recv, join_send, join_recv, wide_send, wide_recv,
):
    me, ch = lax.axis_index("ctx"), lax.axis_index("ch")
    z, x = me // 2, me % 2
    twin = me + 1 - 2 * x
    y, core = ch // 2, ch % 2
    across = (1 - y) * 2 + core
    mate = y * 2 + 1 - core
    length = cot_ref.shape[0]
    piece = turned_ref.shape[1]
    greet(
        [ctx_id(lax.rem(me + d, 8)) for d in range(1, 8)]
        + [ch_id(lax.rem(ch + d, 4)) for d in range(1, 4)]
    )
    first, rest = pl.ds(0, cut), pl.ds(cut, length - cut)

    turns = []
    for d in range(1, 4):
        to = lax.rem(ch + d, 4)
        came = lax.rem(ch + 4 - d, 4)
        for h in range(2):
            slot = 2 * d + h
            out = remote(
                gated_ref.at[h, to], turned_ref.at[2 * ch + h], turn_send.at[slot], turn_recv.at[slot], ch_id(to)
            )
            out.start()
            back = remote(
                gated_ref.at[h, to], turned_ref.at[2 * came + h], turn_send.at[slot], turn_recv.at[slot], ch_id(to)
            )
            turns.append((out, back))
    locals_ = [pltpu.make_async_copy(gated_ref.at[h, ch], turned_ref.at[2 * ch + h], own_sem.at[h]) for h in range(2)]
    locals_.append(pltpu.make_async_copy(cot_ref, cots_ref.at[me], own_sem.at[2]))

    def to_twin_first():
        return remote(cot_ref.at[first], cots_ref.at[me, first], p_send.at[0], g_recv.at[z], ctx_id(twin))

    def to_twin_rest(origin, src):
        slot = 2 * origin + x
        return remote(src, cots_ref.at[slot, rest], q_send.at[origin], q_recv.at[origin], ctx_id(twin))

    def along(origin, side, src):
        slot = 2 * origin + x
        to = me + 2 * side
        return remote(src, cots_ref.at[slot], f_send.at[(side + 1) // 2, origin], f_recv.at[origin], ctx_id(to))

    def along_first(origin, side):
        slot = 2 * origin + 1 - x
        to = me + 2 * side
        part = cots_ref.at[slot, first]
        return remote(part, part, g_send.at[(side + 1) // 2, origin], g_recv.at[origin], ctx_id(to))

    def goes(side):
        return z < 3 if side > 0 else z > 0

    to_twin_first().start()
    for side in (1, -1):

        @pl.when(goes(side))
        def _():
            along(z, side, cot_ref).start()

    to_twin_rest(z, cot_ref.at[rest]).start()
    for copy in locals_:
        copy.start()

    for copy in locals_[:2]:
        copy.wait()
    for out, back in turns:
        back.wait_recv()

    columns = pl.ds(pl.multiple_of(me * length, 128), length)
    mine = pl.ds(pl.multiple_of(ch * piece, piece), piece)
    joins = []
    for d in range(1, 8):
        to = lax.rem(me + d, 8)
        came = lax.rem(me + 8 - d, 8)
        from_columns = pl.ds(pl.multiple_of(came * length, 128), length)
        out = remote(turned_ref.at[to], joined_ref.at[:, columns], join_send.at[d], join_recv.at[d], ctx_id(to))
        out.start()
        back = remote(
            turned_ref.at[to], joined_ref.at[:, from_columns], join_send.at[d], join_recv.at[d], ctx_id(to)
        )
        joins.append((out, back))
    own_join = pltpu.make_async_copy(turned_ref.at[me], joined_ref.at[:, columns], own_sem.at[3])
    own_join.start()

    remote(
        cot_ref.at[first], cots_ref.at[twin, first], p_send.at[0], g_recv.at[z], ctx_id(twin)
    ).wait_recv()
    for side in (1, -1):

        @pl.when(goes(side))
        def _():
            along_first(z, side).start()

    def step(s):
        for side in (1, -1):
            origin = z - side * s

            @pl.when((origin >= 0) & (origin <= 3))
            def _():
                slot = 2 * origin + x
                arrived = cots_ref.at[slot]
                along(origin, side, arrived).wait_recv()

                @pl.when(goes(side))
                def _():
                    along(origin, side, arrived).start()

                to_twin_rest(origin, cots_ref.at[slot, rest]).start()

        for side in (1, -1):
            origin = z - side * s

            @pl.when((origin >= 0) & (origin <= 3))
            def _():
                along_first(origin, side).wait_recv()

                @pl.when(goes(side))
                def _():
                    along_first(origin, side).start()

    step(1)
    own_join.wait()
    for out, back in joins:
        back.wait_recv()

    def rows_of(index):
        return rows_ref.at[pl.ds(pl.multiple_of(index * piece, piece), piece)]

    wide_across = remote(joined_ref, rows_of(ch), wide_send.at[0], wide_recv.at[0], ch_id(across))
    wide_mate = remote(joined_ref, rows_of(ch), wide_send.at[1], wide_recv.at[1], ch_id(mate))
    wide_own = pltpu.make_async_copy(joined_ref, rows_of(ch), own_sem.at[4])
    wide_across.start()
    wide_mate.start()
    wide_own.start()
    step(2)
    remote(joined_ref, rows_of(across), wide_send.at[0], wide_recv.at[0], ch_id(across)).wait_recv()
    wide_on = remote(rows_of(across), rows_of(across), wide_send.at[2], wide_recv.at[2], ch_id(mate))
    wide_on.start()
    step(3)

    remote(joined_ref, rows_of(mate), wide_send.at[1], wide_recv.at[1], ch_id(mate)).wait_recv()
    far = (1 - y) * 2 + 1 - core
    remote(rows_of(across), rows_of(far), wide_send.at[2], wide_recv.at[2], ch_id(mate)).wait_recv()
    for origin in range(4):
        slot = 2 * origin + 1 - x
        part = cots_ref.at[slot, rest]
        remote(part, part, q_send.at[origin], q_recv.at[origin], ctx_id(twin)).wait_recv()
    to_twin_first().wait_send()
    for origin in range(4):
        to_twin_rest(origin, cot_ref.at[rest]).wait_send()
        for side in (1, -1):

            @pl.when(goes(side) & (origin <= z if side > 0 else origin >= z))
            def _():
                along(origin, side, cot_ref).wait_send()
                along_first(origin, side).wait_send()

    for out, back in turns + joins:
        out.wait_send()
    wide_across.wait_send()
    wide_mate.wait_send()
    wide_on.wait_send()
    wide_own.wait()
    locals_[2].wait()


def move_all(gated, cotangent):
    n_ctx, n_ch = lax.axis_size("ctx"), lax.axis_size("ch")
    rows, length = gated.shape
    if (n_ctx, n_ch) != (8, 4) or rows % (2 * n_ch * 16) or length % 128:
        return (
            exchange_rows(gated, n_ctx, n_ch),
            lax.all_gather(cotangent, "ctx", axis=0, tiled=True),
        )
    piece = rows // 2 // n_ch
    width = cotangent.shape[1]
    any_space = pl.BlockSpec(memory_space=pl.ANY)
    bf16 = jnp.bfloat16
    dma = pltpu.SemaphoreType.DMA
    cots, gathered, _, _ = pl.pallas_call(
        functools.partial(move_kernel, CUT),
        out_shape=(
            jax.ShapeDtypeStruct((n_ctx, length, width), bf16),
            jax.ShapeDtypeStruct((rows // 2, n_ctx * length), bf16),
            jax.ShapeDtypeStruct((n_ctx, piece, length), bf16),
            jax.ShapeDtypeStruct((piece, n_ctx * length), bf16),
        ),
        in_specs=[any_space] * 2,
        out_specs=[any_space] * 4,
        scratch_shapes=[
            dma((5,)), dma((4,)), dma((4,)), dma((4,)), dma((2, 4)), dma((2, 4)), dma((1,)), dma((4,)),
            dma((8,)), dma((8,)), dma((8,)), dma((8,)), dma((3,)), dma((3,)),
        ],
        compiler_params=pltpu.CompilerParams(collective_id=2, has_side_effects=True),
        cost_estimate=pl.CostEstimate(flops=0, bytes_accessed=300_000_000, transcendentals=0),
        name="move_all",
    )(cotangent, gated.reshape(2, n_ch, piece, length))
    return gathered, cots.reshape(n_ctx * length, width)


def local(
    query_input, key_input, value_input, decay_rate, residue, doc_ends, out_weight, out_cotangent
):
    rows_here, length = query_input.shape
    n_ctx, n_ch = lax.axis_size("ctx"), lax.axis_size("ch")
    groups = decay_rate.shape[0]
    group_rows = rows_here // groups
    me = lax.axis_index("ctx")
    offsets = jnp.arange(length, dtype=jnp.int32)
    place = offsets.astype(jnp.float32)
    doc_ids = doc_of(doc_ends, me * length + offsets)
    blocks = jnp.arange(n_ctx, dtype=jnp.int32)
    last_ids = doc_of(doc_ends, (blocks + 1) * length - 1)
    previous = jnp.where(me > 0, jnp.sum((doc_ends <= me * length - 1).astype(jnp.int32)), -1)
    last = doc_ids[-1]

    alive_mask = (doc_ids == previous).astype(jnp.float32)
    tail_mask = (doc_ids == last).astype(jnp.float32)
    rate = decay_rate[:, :, None]
    carry_in_map = residue[:, :, None] * jnp.exp(-rate * (place + 1.0)) * alive_mask
    carry_out_map = jnp.exp(-rate * (length - 1.0 - place)) * tail_mask
    back_out_map = jnp.exp(-rate * place) * alive_mask
    back_in_map = residue[:, :, None] * jnp.exp(-rate * (length - place)) * tail_mask
    steps_ahead = me - 1 - blocks
    joined_ahead = (steps_ahead >= 0) & (last_ids == previous)
    ahead_weight = jnp.where(
        joined_ahead[:, None, None],
        jnp.exp(-decay_rate[None] * (length * jnp.maximum(steps_ahead, 0)).astype(jnp.float32)[:, None, None]),
        0.0,
    )
    steps_back = blocks - 1 - me
    before_ids = jnp.concatenate([jnp.full((1,), -1, jnp.int32), last_ids[:-1]])
    joined_back = (steps_back >= 0) & (before_ids == last)
    back_weight = jnp.where(
        joined_back[:, None, None],
        jnp.exp(-decay_rate[None] * (length * jnp.maximum(steps_back, 0)).astype(jnp.float32)[:, None, None]),
        0.0,
    )

    key_f = key_input.astype(jnp.float32)
    value_f = value_input.astype(jnp.float32)
    query_f = query_input.astype(jnp.float32)
    mixed = (key_f * value_f).reshape(groups, group_rows, length)
    forward_part = jnp.einsum("gnl,gcl->gnc", carry_out_map, mixed, precision=HIGH)
    forward_all = spread_states(forward_part, 1, 0)
    entering = jnp.sum(
        jnp.where(joined_ahead[:, None, None, None], ahead_weight[..., None] * forward_all, 0.0), axis=0
    )

    partial_grad = lax.dot_general(
        out_weight, out_cotangent, (((1,), (1,)), ((), ())), preferred_element_type=jnp.float32
    )
    output_grad = lax.psum_scatter(partial_grad, "ch", scatter_dimension=0, tiled=True)

    kernel = local_kernel(decay_rate, residue, doc_ids, length)
    filtered = jnp.einsum("gcs,gts->gct", mixed, kernel, precision=HIGH)
    filtered = filtered + jnp.einsum("gnc,gnt->gct", entering, carry_in_map, precision=HIGH)
    filtered = filtered.reshape(rows_here, length)
    gated = (query_f * filtered).astype(jnp.bfloat16)
    gated_rows, cotangent_all = move_all(gated, out_cotangent)
    output_grad, gated_rows, cotangent_all = lax.optimization_barrier((output_grad, gated_rows, cotangent_all))

    signal = (output_grad * query_f).reshape(groups, group_rows, length)
    backward_part = jnp.einsum("gnl,gcl->gnc", back_out_map, signal, precision=HIGH)
    backward_all = spread_states(backward_part, -1, 1)
    query_grad = (output_grad * filtered).astype(jnp.bfloat16)
    spread = jnp.einsum("gct,gts->gcs", signal, kernel, precision=HIGH)
    returning = jnp.sum(
        jnp.where(joined_back[:, None, None, None], back_weight[..., None] * backward_all, 0.0), axis=0
    )
    spread = spread + jnp.einsum("gnc,gns->gcs", returning, back_in_map, precision=HIGH)
    spread = spread.reshape(rows_here, length)
    key_grad = (spread * value_f).astype(jnp.bfloat16)
    value_grad = (spread * key_f).astype(jnp.bfloat16)

    norm_factor = 1.0 / math.sqrt(length * n_ctx)
    weight_grad = jnp.dot(gated_rows, cotangent_all, preferred_element_type=jnp.float32) * norm_factor
    return (query_grad, key_grad, value_grad, weight_grad)


def solution(mesh):
    return jax.shard_map(
        local,
        mesh=mesh,
        in_specs=(
            P("ch", "ctx"),
            P("ch", "ctx"),
            P("ch", "ctx"),
            P("ch", None),
            P("ch", None),
            P(),
            P(None, "ch"),
            P("ctx", "ch"),
        ),
        out_specs=(P("ch", "ctx"), P("ch", "ctx"), P("ch", "ctx"), P("ctx", "ch")),
        check_vma=False,
    )
```

```python
import functools
import math

import jax
import jax.numpy as jnp
from jax import lax
from jax.experimental import pallas as pl
from jax.experimental.pallas import tpu as pltpu
from jax.sharding import PartitionSpec as P

MESH = pl.DeviceIdType.MESH
HIGH = lax.Precision.HIGH
TILE = 128
CUT = 96


def doc_of(doc_ends, positions):
    return jnp.sum((doc_ends[None, :] <= positions[:, None]).astype(jnp.int32), axis=1)


def local_kernel(decay_rate, residue, doc_ids, length):
    groups = decay_rate.shape[0]
    place = jnp.arange(length, dtype=jnp.float32)
    narrow = jnp.arange(TILE, dtype=jnp.float32)
    half = 0.5 * TILE
    rising = jnp.exp(-decay_rate[:, None, :] * (place - half)[None, :, None]) * residue[:, None, :]
    falling = jnp.exp(decay_rate[:, None, :] * (narrow - half)[None, :, None])
    strip = jnp.einsum("gtn,gsn->gts", rising, falling, precision=lax.Precision.HIGHEST)
    columns = []
    for start in range(0, length, TILE):
        top = jnp.zeros((groups, start, TILE), jnp.float32)
        columns.append(jnp.concatenate([top, strip[:, : length - start]], axis=1))
    kernel = jnp.concatenate(columns, axis=2)
    offsets = jnp.arange(length, dtype=jnp.int32)
    causal = (offsets[:, None] >= offsets[None, :]) & (doc_ids[:, None] == doc_ids[None, :])
    return jnp.where(causal[None], kernel, 0.0)


def exchange_rows(gated, n_ctx, n_ch):
    rows, length = gated.shape
    mine = rows * n_ch // n_ctx
    pieces = gated.reshape(n_ctx // n_ch, n_ch, mine // n_ch, length)
    pieces = lax.all_to_all(pieces, "ch", split_axis=1, concat_axis=0, tiled=True)
    pieces = pieces.reshape(n_ctx, mine // n_ch, length)
    pieces = lax.all_to_all(pieces, "ctx", split_axis=0, concat_axis=0, tiled=True)
    pieces = pieces.transpose(1, 0, 2).reshape(mine // n_ch, n_ctx * length)
    return lax.all_gather(pieces, "ch", axis=0, tiled=True)


def ctx_id(index):
    return (index, lax.axis_index("ch"))


def ch_id(index):
    return (lax.axis_index("ctx"), index)


def remote(src, dst, send, recv, device):
    return pltpu.make_async_remote_copy(
        src_ref=src, dst_ref=dst, send_sem=send, recv_sem=recv, device_id=device, device_id_type=MESH
    )


def greet(devices):
    barrier = pltpu.get_barrier_semaphore()
    for device in devices:
        pl.semaphore_signal(barrier, inc=1, device_id=device, device_id_type=MESH)
    pl.semaphore_wait(barrier, len(devices))


def inside(index):
    return (index >= 0) & (index < 8)


def state_copies(part, slots, send, recv, sign):
    me = lax.axis_index("ctx")
    for d in range(1, 8):
        to = me + sign * d

        @pl.when(inside(to))
        def _():
            remote(part, slots.at[me], send.at[d], recv.at[d], ctx_id(to)).start()

    def arrive():
        for d in range(1, 8):
            came = me - sign * d

            @pl.when(inside(came))
            def _():
                remote(part, slots.at[came], send.at[d], recv.at[d], ctx_id(came)).wait_recv()

    def sent():
        for d in range(1, 8):
            to = me + sign * d

            @pl.when(inside(to))
            def _():
                remote(part, slots.at[me], send.at[d], recv.at[d], ctx_id(to)).wait_send()

    return arrive, sent


def weigh(total, weight, slots, sign):
    me = lax.axis_index("ctx")
    total[...] = jnp.zeros_like(total)
    for k in range(8):

        @pl.when(k < me if sign > 0 else k > me)
        def _():
            total[...] += weight[k] * slots[k]


def move_kernel(
    cut, cot_ref, partial_ref, part_ref, near_ref, query_ref, ahead_ref, behind_ref, in_map_ref, out_map_ref,
    cots_ref, rows_ref, turned_ref, joined_ref, signal_ref, query_grad_ref, returning_ref,
    ahead_slots, back_slots, back_part, entering, filtered_ref, gated_ref, halves, arrived_halves, last_half,
    ahead_send, ahead_recv, back_send, back_recv, half_sem, half_send, half_recv, last_send, last_recv,
    own_sem, f_recv, g_recv, q_recv, f_send, g_send, p_send, q_send,
    turn_send, turn_recv, join_send, join_recv, wide_send, wide_recv,
):
    me, ch = lax.axis_index("ctx"), lax.axis_index("ch")
    z, x = me // 2, me % 2
    twin = me + 1 - 2 * x
    y, core = ch // 2, ch % 2
    across = (1 - y) * 2 + core
    mate = y * 2 + 1 - core
    far = (1 - y) * 2 + 1 - core
    length = cot_ref.shape[0]
    piece = turned_ref.shape[1]
    group_rows = 4 * piece
    greet(
        [ctx_id(lax.rem(me + d, 8)) for d in range(1, 8)]
        + [ch_id(lax.rem(ch + d, 4)) for d in range(1, 4)]
    )
    first, rest = pl.ds(0, cut), pl.ds(cut, length - cut)
    ahead_arrive, ahead_sent = state_copies(part_ref, ahead_slots, ahead_send, ahead_recv, 1)

    to_mate = [
        remote(partial_ref.at[index], arrived_halves.at[k], half_send.at[k], half_recv.at[k], ch_id(mate))
        for k, index in ((0, far), (1, mate))
    ]
    own_halves = [
        pltpu.make_async_copy(partial_ref.at[index], halves.at[k], half_sem.at[k])
        for k, index in ((0, across), (1, ch))
    ]
    cot_copy = pltpu.make_async_copy(cot_ref, cots_ref.at[me], own_sem.at[2])

    def to_twin_first():
        return remote(cot_ref.at[first], cots_ref.at[me, first], p_send.at[0], g_recv.at[z], ctx_id(twin))

    def to_twin_rest(origin, src):
        slot = 2 * origin + x
        return remote(src, cots_ref.at[slot, rest], q_send.at[origin], q_recv.at[origin], ctx_id(twin))

    def along(origin, side, src):
        slot = 2 * origin + x
        to = me + 2 * side
        return remote(src, cots_ref.at[slot], f_send.at[(side + 1) // 2, origin], f_recv.at[origin], ctx_id(to))

    def along_first(origin, side):
        slot = 2 * origin + 1 - x
        to = me + 2 * side
        part = cots_ref.at[slot, first]
        return remote(part, part, g_send.at[(side + 1) // 2, origin], g_recv.at[origin], ctx_id(to))

    def goes(side):
        return z < 3 if side > 0 else z > 0

    to_twin_first().start()
    for side in (1, -1):

        @pl.when(goes(side))
        def _():
            along(z, side, cot_ref).start()

    to_twin_rest(z, cot_ref.at[rest]).start()
    for copy in to_mate + own_halves + [cot_copy]:
        copy.start()

    ahead_arrive()
    weigh(entering, ahead_ref, ahead_slots, 1)
    for g in range(2):
        carried = entering[g].T

        for r in range(4):
            rows = pl.ds(g * group_rows + r * piece, piece)
            filtered = near_ref[rows, :] + jnp.dot(
                carried[r * piece : (r + 1) * piece],
                in_map_ref[g],
                precision=lax.Precision.HIGHEST,
                preferred_element_type=jnp.float32,
            )
            filtered_ref[rows, :] = filtered
            gated_ref[g, r] = (query_ref[rows, :].astype(jnp.float32) * filtered).astype(jnp.bfloat16)

    turns = []
    for d in range(1, 4):
        to = lax.rem(ch + d, 4)
        came = lax.rem(ch + 4 - d, 4)
        for h in range(2):
            slot = 2 * d + h
            out = remote(
                gated_ref.at[h, to], turned_ref.at[2 * ch + h], turn_send.at[slot], turn_recv.at[slot], ch_id(to)
            )
            out.start()
            back = remote(
                gated_ref.at[h, to], turned_ref.at[2 * came + h], turn_send.at[slot], turn_recv.at[slot], ch_id(to)
            )
            turns.append((out, back))
    own_turns = [
        pltpu.make_async_copy(gated_ref.at[h, ch], turned_ref.at[2 * ch + h], own_sem.at[h]) for h in range(2)
    ]
    for copy in own_turns:
        copy.start()

    own_halves[0].wait()
    to_mate[0].wait_recv()

    @pl.loop(0, 8)
    def _(r):
        rows = pl.ds(pl.multiple_of(r * piece, piece), piece)
        halves[0, rows, :] += arrived_halves[0, rows, :]

    to_across = remote(halves.at[0], last_half, last_send.at[0], last_recv.at[0], ch_id(across))
    to_across.start()

    for copy in own_turns:
        copy.wait()
    for out, back in turns:
        back.wait_recv()

    columns = pl.ds(pl.multiple_of(me * length, 128), length)
    mine = pl.ds(pl.multiple_of(ch * piece, piece), piece)
    joins = []
    for d in range(1, 8):
        to = lax.rem(me + d, 8)
        came = lax.rem(me + 8 - d, 8)
        from_columns = pl.ds(pl.multiple_of(came * length, 128), length)
        out = remote(turned_ref.at[to], joined_ref.at[:, columns], join_send.at[d], join_recv.at[d], ctx_id(to))
        out.start()
        back = remote(
            turned_ref.at[to], joined_ref.at[:, from_columns], join_send.at[d], join_recv.at[d], ctx_id(to)
        )
        joins.append((out, back))
    own_join = pltpu.make_async_copy(turned_ref.at[me], joined_ref.at[:, columns], own_sem.at[3])
    own_join.start()

    remote(
        cot_ref.at[first], cots_ref.at[twin, first], p_send.at[0], g_recv.at[z], ctx_id(twin)
    ).wait_recv()
    for side in (1, -1):

        @pl.when(goes(side))
        def _():
            along_first(z, side).start()

    def step(s):
        for side in (1, -1):
            origin = z - side * s

            @pl.when((origin >= 0) & (origin <= 3))
            def _():
                slot = 2 * origin + x
                arrived = cots_ref.at[slot]
                along(origin, side, arrived).wait_recv()

                @pl.when(goes(side))
                def _():
                    along(origin, side, arrived).start()

                to_twin_rest(origin, cots_ref.at[slot, rest]).start()

        for side in (1, -1):
            origin = z - side * s

            @pl.when((origin >= 0) & (origin <= 3))
            def _():
                along_first(origin, side).wait_recv()

                @pl.when(goes(side))
                def _():
                    along_first(origin, side).start()

    step(1)
    own_join.wait()
    for out, back in joins:
        back.wait_recv()

    def rows_of(index):
        return rows_ref.at[pl.ds(pl.multiple_of(index * piece, piece), piece)]

    wide_across = remote(joined_ref, rows_of(ch), wide_send.at[0], wide_recv.at[0], ch_id(across))
    wide_mate = remote(joined_ref, rows_of(ch), wide_send.at[1], wide_recv.at[1], ch_id(mate))
    wide_own = pltpu.make_async_copy(joined_ref, rows_of(ch), own_sem.at[4])
    wide_across.start()
    wide_mate.start()
    wide_own.start()
    step(2)
    remote(joined_ref, rows_of(across), wide_send.at[0], wide_recv.at[0], ch_id(across)).wait_recv()
    wide_on = remote(rows_of(across), rows_of(across), wide_send.at[2], wide_recv.at[2], ch_id(mate))
    wide_on.start()
    own_halves[1].wait()
    to_mate[1].wait_recv()
    to_across.wait_recv()
    for g in range(2):

        @pl.loop(0, 4)
        def _(r):
            rows = pl.ds(pl.multiple_of(g * group_rows + r * piece, piece), piece)
            output_grad = halves[1, rows, :] + arrived_halves[1, rows, :] + last_half[rows, :]
            signal_ref[rows, :] = output_grad * query_ref[rows, :].astype(jnp.float32)
            query_grad_ref[rows, :] = (output_grad * filtered_ref[rows, :]).astype(jnp.bfloat16)

        back_part[g] = lax.dot_general(
            out_map_ref[g],
            signal_ref[pl.ds(g * group_rows, group_rows), :],
            (((1,), (1,)), ((), ())),
            precision=lax.Precision.HIGHEST,
            preferred_element_type=jnp.float32,
        )
    back_arrive, back_sent = state_copies(back_part, back_slots, back_send, back_recv, -1)
    step(3)
    back_arrive()
    weigh(returning_ref, behind_ref, back_slots, -1)

    remote(joined_ref, rows_of(mate), wide_send.at[1], wide_recv.at[1], ch_id(mate)).wait_recv()
    remote(rows_of(across), rows_of(far), wide_send.at[2], wide_recv.at[2], ch_id(mate)).wait_recv()
    for origin in range(4):
        slot = 2 * origin + 1 - x
        part = cots_ref.at[slot, rest]
        remote(part, part, q_send.at[origin], q_recv.at[origin], ctx_id(twin)).wait_recv()
    to_twin_first().wait_send()
    for origin in range(4):
        to_twin_rest(origin, cot_ref.at[rest]).wait_send()
        for side in (1, -1):

            @pl.when(goes(side) & (origin <= z if side > 0 else origin >= z))
            def _():
                along(origin, side, cot_ref).wait_send()
                along_first(origin, side).wait_send()

    for out, back in turns + joins:
        out.wait_send()
    wide_across.wait_send()
    wide_mate.wait_send()
    wide_on.wait_send()
    wide_own.wait()
    cot_copy.wait()
    for copy in to_mate + [to_across]:
        copy.wait_send()
    ahead_sent()
    back_sent()


def move_all(cotangent, partial_grad, part, near, query, ahead, behind, in_map, out_map):
    n_ctx, n_ch = lax.axis_size("ctx"), lax.axis_size("ch")
    rows, length = query.shape
    piece = rows // 2 // n_ch
    width = cotangent.shape[1]
    any_space = pl.BlockSpec(memory_space=pl.ANY)
    vmem = pl.BlockSpec(memory_space=pltpu.VMEM)
    f32, bf16 = jnp.float32, jnp.bfloat16
    dma = pltpu.SemaphoreType.DMA
    cots, gathered, _, _, signal, query_grad, returning = pl.pallas_call(
        functools.partial(move_kernel, CUT),
        out_shape=(
            jax.ShapeDtypeStruct((n_ctx, length, width), bf16),
            jax.ShapeDtypeStruct((rows // 2, n_ctx * length), bf16),
            jax.ShapeDtypeStruct((n_ctx, piece, length), bf16),
            jax.ShapeDtypeStruct((piece, n_ctx * length), bf16),
            jax.ShapeDtypeStruct((rows, length), f32),
            jax.ShapeDtypeStruct((rows, length), bf16),
            jax.ShapeDtypeStruct(part.shape, f32),
        ),
        in_specs=[any_space, any_space] + [vmem] * 7,
        out_specs=[any_space] * 4 + [vmem] * 3,
        scratch_shapes=[
            pltpu.VMEM((n_ctx,) + part.shape, f32),
            pltpu.VMEM((n_ctx,) + part.shape, f32),
            pltpu.VMEM(part.shape, f32),
            pltpu.VMEM(part.shape, f32),
            pltpu.VMEM((rows, length), f32),
            pltpu.VMEM((2, n_ch, piece, length), bf16),
            pltpu.VMEM((2, rows, length), f32),
            pltpu.VMEM((2, rows, length), f32),
            pltpu.VMEM((rows, length), f32),
            dma((8,)), dma((8,)), dma((8,)), dma((8,)), dma((2,)), dma((2,)), dma((2,)), dma((1,)), dma((1,)),
            dma((5,)), dma((4,)), dma((4,)), dma((4,)), dma((2, 4)), dma((2, 4)), dma((1,)), dma((4,)),
            dma((8,)), dma((8,)), dma((8,)), dma((8,)), dma((3,)), dma((3,)),
        ],
        compiler_params=pltpu.CompilerParams(
            collective_id=0, has_side_effects=True, vmem_limit_bytes=48 * 1024 * 1024
        ),
        cost_estimate=pl.CostEstimate(flops=0, bytes_accessed=300_000_000, transcendentals=0),
        name="move_all",
    )(cotangent, partial_grad.reshape(n_ch, rows, length), part, near, query, ahead, behind, in_map, out_map)
    return signal, query_grad, returning, gathered, cots.reshape(n_ctx * length, width)


def move_by_collectives(cotangent, partial_grad, part, near, query, ahead, behind, in_map, out_map):
    n_ctx, n_ch = lax.axis_size("ctx"), lax.axis_size("ch")
    groups = part.shape[0]
    rows, length = query.shape
    query_f = query.astype(jnp.float32)
    cots = lax.all_gather(cotangent, "ctx", axis=0, tiled=True)
    output_grad = lax.psum_scatter(partial_grad, "ch", scatter_dimension=0, tiled=True)
    entering = jnp.sum(ahead * lax.all_gather(part, "ctx", axis=0), axis=0)
    carried = jnp.einsum("gnc,gnt->gct", entering, in_map, precision=HIGH).reshape(rows, length)
    filtered = near + carried
    gathered = exchange_rows((query_f * filtered).astype(jnp.bfloat16), n_ctx, n_ch)
    signal = output_grad * query_f
    back_part = jnp.einsum("gnl,gcl->gnc", out_map, signal.reshape(groups, rows // groups, length), precision=HIGH)
    returning = jnp.sum(behind * lax.all_gather(back_part, "ctx", axis=0), axis=0)
    query_grad = (output_grad * filtered).astype(jnp.bfloat16)
    return signal, query_grad, returning, gathered, cots


def local(
    query_input, key_input, value_input, decay_rate, residue, doc_ends, out_weight, out_cotangent
):
    rows_here, length = query_input.shape
    n_ctx, n_ch = lax.axis_size("ctx"), lax.axis_size("ch")
    groups = decay_rate.shape[0]
    group_rows = rows_here // groups
    me = lax.axis_index("ctx")
    offsets = jnp.arange(length, dtype=jnp.int32)
    place = offsets.astype(jnp.float32)
    doc_ids = doc_of(doc_ends, me * length + offsets)
    blocks = jnp.arange(n_ctx, dtype=jnp.int32)
    last_ids = doc_of(doc_ends, (blocks + 1) * length - 1)
    previous = jnp.where(me > 0, jnp.sum((doc_ends <= me * length - 1).astype(jnp.int32)), -1)
    last = doc_ids[-1]

    alive_mask = (doc_ids == previous).astype(jnp.float32)
    tail_mask = (doc_ids == last).astype(jnp.float32)
    rate = decay_rate[:, :, None]
    carry_in_map = residue[:, :, None] * jnp.exp(-rate * (place + 1.0)) * alive_mask
    carry_out_map = jnp.exp(-rate * (length - 1.0 - place)) * tail_mask
    back_out_map = jnp.exp(-rate * place) * alive_mask
    back_in_map = residue[:, :, None] * jnp.exp(-rate * (length - place)) * tail_mask
    steps_ahead = me - 1 - blocks
    joined_ahead = (steps_ahead >= 0) & (last_ids == previous)
    ahead_weight = jnp.where(
        joined_ahead[:, None, None],
        jnp.exp(-decay_rate[None] * (length * jnp.maximum(steps_ahead, 0)).astype(jnp.float32)[:, None, None]),
        0.0,
    )
    steps_back = blocks - 1 - me
    before_ids = jnp.concatenate([jnp.full((1,), -1, jnp.int32), last_ids[:-1]])
    joined_back = (steps_back >= 0) & (before_ids == last)
    back_weight = jnp.where(
        joined_back[:, None, None],
        jnp.exp(-decay_rate[None] * (length * jnp.maximum(steps_back, 0)).astype(jnp.float32)[:, None, None]),
        0.0,
    )

    key_f = key_input.astype(jnp.float32)
    value_f = value_input.astype(jnp.float32)
    mixed = (key_f * value_f).reshape(groups, group_rows, length)
    forward_part = jnp.einsum("gnl,gcl->gnc", carry_out_map, mixed, precision=HIGH)
    partial_grad = lax.dot_general(
        out_weight, out_cotangent, (((1,), (1,)), ((), ())), preferred_element_type=jnp.float32
    )

    kernel = local_kernel(decay_rate, residue, doc_ids, length)
    near = jnp.einsum("gcs,gts->gct", mixed, kernel, precision=HIGH).reshape(rows_here, length)
    wide = (n_ctx,) + forward_part.shape
    on_kernel = (n_ctx, n_ch, groups) == (8, 4, 2) and rows_here == 1024 and length == 512
    move = move_all if on_kernel else move_by_collectives
    signal, query_grad, returning, gated_rows, cotangent_all = move(
        out_cotangent,
        partial_grad,
        forward_part,
        near,
        query_input,
        jnp.broadcast_to(ahead_weight[..., None], wide),
        jnp.broadcast_to(back_weight[..., None], wide),
        carry_in_map,
        back_out_map,
    )
    signal = signal.reshape(groups, group_rows, length)
    spread = jnp.einsum("gct,gts->gcs", signal, kernel, precision=HIGH)
    spread = spread + jnp.einsum("gnc,gns->gcs", returning, back_in_map, precision=HIGH)
    spread = spread.reshape(rows_here, length)
    key_grad = (spread * value_f).astype(jnp.bfloat16)
    value_grad = (spread * key_f).astype(jnp.bfloat16)

    norm_factor = 1.0 / math.sqrt(length * n_ctx)
    weight_grad = jnp.dot(gated_rows, cotangent_all, preferred_element_type=jnp.float32) * norm_factor
    return (query_grad, key_grad, value_grad, weight_grad)


def solution(mesh):
    return jax.shard_map(
        local,
        mesh=mesh,
        in_specs=(
            P("ch", "ctx"),
            P("ch", "ctx"),
            P("ch", "ctx"),
            P("ch", None),
            P("ch", None),
            P(),
            P(None, "ch"),
            P("ctx", "ch"),
        ),
        out_specs=(P("ch", "ctx"), P("ch", "ctx"), P("ch", "ctx"), P("ctx", "ch")),
        check_vma=False,
    )
```

```python
import functools
import math

import jax
import jax.numpy as jnp
from jax import lax
from jax.experimental import pallas as pl
from jax.experimental.pallas import tpu as pltpu
from jax.sharding import PartitionSpec as P

MESH = pl.DeviceIdType.MESH
HIGH = lax.Precision.HIGH
TILE = 128
CUT = 96


def doc_of(doc_ends, positions):
    return jnp.sum((doc_ends[None, :] <= positions[:, None]).astype(jnp.int32), axis=1)


def local_kernel(decay_rate, residue, doc_ids, length):
    groups = decay_rate.shape[0]
    place = jnp.arange(length, dtype=jnp.float32)
    narrow = jnp.arange(TILE, dtype=jnp.float32)
    half = 0.5 * TILE
    rising = jnp.exp(-decay_rate[:, None, :] * (place - half)[None, :, None]) * residue[:, None, :]
    falling = jnp.exp(decay_rate[:, None, :] * (narrow - half)[None, :, None])
    strip = jnp.einsum("gtn,gsn->gts", rising, falling, precision=lax.Precision.HIGHEST)
    columns = []
    for start in range(0, length, TILE):
        top = jnp.zeros((groups, start, TILE), jnp.float32)
        columns.append(jnp.concatenate([top, strip[:, : length - start]], axis=1))
    kernel = jnp.concatenate(columns, axis=2)
    offsets = jnp.arange(length, dtype=jnp.int32)
    causal = (offsets[:, None] >= offsets[None, :]) & (doc_ids[:, None] == doc_ids[None, :])
    return jnp.where(causal[None], kernel, 0.0)


def exchange_rows(gated, n_ctx, n_ch):
    rows, length = gated.shape
    mine = rows * n_ch // n_ctx
    pieces = gated.reshape(n_ctx // n_ch, n_ch, mine // n_ch, length)
    pieces = lax.all_to_all(pieces, "ch", split_axis=1, concat_axis=0, tiled=True)
    pieces = pieces.reshape(n_ctx, mine // n_ch, length)
    pieces = lax.all_to_all(pieces, "ctx", split_axis=0, concat_axis=0, tiled=True)
    pieces = pieces.transpose(1, 0, 2).reshape(mine // n_ch, n_ctx * length)
    return lax.all_gather(pieces, "ch", axis=0, tiled=True)


def ctx_id(index):
    return (index, lax.axis_index("ch"))


def ch_id(index):
    return (lax.axis_index("ctx"), index)


def remote(src, dst, send, recv, device):
    return pltpu.make_async_remote_copy(
        src_ref=src, dst_ref=dst, send_sem=send, recv_sem=recv, device_id=device, device_id_type=MESH
    )


def greet(devices):
    barrier = pltpu.get_barrier_semaphore()
    for device in devices:
        pl.semaphore_signal(barrier, inc=1, device_id=device, device_id_type=MESH)
    pl.semaphore_wait(barrier, len(devices))


def inside(index):
    return (index >= 0) & (index < 8)


def state_copies(part, slots, send, recv, sign):
    me = lax.axis_index("ctx")
    for d in range(1, 8):
        to = me + sign * d

        @pl.when(inside(to))
        def _():
            remote(part, slots.at[me], send.at[d], recv.at[d], ctx_id(to)).start()

    def arrive():
        for d in range(1, 8):
            came = me - sign * d

            @pl.when(inside(came))
            def _():
                remote(part, slots.at[came], send.at[d], recv.at[d], ctx_id(came)).wait_recv()

    def sent():
        for d in range(1, 8):
            to = me + sign * d

            @pl.when(inside(to))
            def _():
                remote(part, slots.at[me], send.at[d], recv.at[d], ctx_id(to)).wait_send()

    return arrive, sent


def weigh(total, weight, slots, sign):
    me = lax.axis_index("ctx")
    total[...] = jnp.zeros_like(total)
    for k in range(8):

        @pl.when(k < me if sign > 0 else k > me)
        def _():
            total[...] += weight[k] * slots[k]


def move_kernel(
    cut, cot_ref, weight_ref, cot_near, part_ref, near_ref, query_ref, ahead_ref, behind_ref, in_map_ref, out_map_ref,
    cots_ref, rows_ref, turned_ref, joined_ref, signal_ref, query_grad_ref, returning_ref,
    ahead_slots, back_slots, back_part, entering, filtered_ref, gated_ref, weights, partial_ref, arrived_halves, last_half,
    ahead_send, ahead_recv, back_send, back_recv, half_sem, half_send, half_recv, last_send, last_recv,
    own_sem, f_recv, g_recv, q_recv, f_send, g_send, p_send, q_send,
    turn_send, turn_recv, join_send, join_recv, wide_send, wide_recv,
):
    me, ch = lax.axis_index("ctx"), lax.axis_index("ch")
    z, x = me // 2, me % 2
    twin = me + 1 - 2 * x
    y, core = ch // 2, ch % 2
    across = (1 - y) * 2 + core
    mate = y * 2 + 1 - core
    far = (1 - y) * 2 + 1 - core
    length = cot_ref.shape[0]
    piece = turned_ref.shape[1]
    group_rows = 4 * piece
    greet(
        [ctx_id(lax.rem(me + d, 8)) for d in range(1, 8)]
        + [ch_id(lax.rem(ch + d, 4)) for d in range(1, 4)]
    )
    first = pl.ds(0, cut)
    ahead_arrive, ahead_sent = state_copies(part_ref, ahead_slots, ahead_send, ahead_recv, 1)

    to_mate = [
        remote(partial_ref.at[index], arrived_halves.at[k], half_send.at[k], half_recv.at[k], ch_id(mate))
        for k, index in ((0, far), (1, mate))
    ]
    rows_here = last_half.shape[0]
    load_weights = [
        pltpu.make_async_copy(
            weight_ref.at[pl.ds(pl.multiple_of(index * rows_here, rows_here), rows_here)],
            weights.at[k],
            half_sem.at[k],
        )
        for k, index in enumerate((far, across, mate, ch))
    ]

    def multiply(k, index):
        load_weights[k].wait()

        @pl.loop(0, 4)
        def _(r):
            rows = pl.ds(pl.multiple_of(r * 2 * piece, piece), 2 * piece)
            partial_ref[index, rows, :] = lax.dot_general(
                weights[k, rows, :], cot_near[...], (((1,), (1,)), ((), ())), preferred_element_type=jnp.float32
            )

    cot_copy = pltpu.make_async_copy(cot_ref, cots_ref.at[me], own_sem.at[2])

    def to_twin_first():
        return remote(cot_ref.at[first], cots_ref.at[me, first], p_send.at[0], g_recv.at[z], ctx_id(twin))

    half = length // 2
    along_rows = (pl.ds(0, half), pl.ds(half, half))
    rest_rows = (pl.ds(cut, half - cut), pl.ds(half, half))

    def to_twin_rest(origin, part, src=None):
        rows = rest_rows[part]
        to = cots_ref.at[2 * origin + x, rows]
        src = to if src is None else src.at[rows]
        return remote(src, to, q_send.at[part, origin], q_recv.at[part, origin], ctx_id(twin))

    def along(origin, side, part, src=None):
        rows = along_rows[part]
        to = cots_ref.at[2 * origin + x, rows]
        src = to if src is None else src.at[rows]
        way = (side + 1) // 2
        return remote(src, to, f_send.at[way, part, origin], f_recv.at[part, origin], ctx_id(me + 2 * side))

    def along_first(origin, side):
        slot = 2 * origin + 1 - x
        to = me + 2 * side
        part = cots_ref.at[slot, first]
        return remote(part, part, g_send.at[(side + 1) // 2, origin], g_recv.at[origin], ctx_id(to))

    def goes(side):
        return z < 3 if side > 0 else z > 0

    to_twin_first().start()
    for side in (1, -1):

        @pl.when(goes(side))
        def _():
            for part in range(2):
                along(z, side, part, cot_ref).start()

    for part in range(2):
        to_twin_rest(z, part, cot_ref).start()
    for copy in load_weights + [cot_copy]:
        copy.start()
    multiply(0, far)
    to_mate[0].start()

    ahead_arrive()
    weigh(entering, ahead_ref, ahead_slots, 1)
    for g in range(2):
        carried = entering[g].T

        for r in range(4):
            rows = pl.ds(g * group_rows + r * piece, piece)
            filtered = near_ref[rows, :] + jnp.dot(
                carried[r * piece : (r + 1) * piece],
                in_map_ref[g],
                precision=lax.Precision.HIGHEST,
                preferred_element_type=jnp.float32,
            )
            filtered_ref[rows, :] = filtered
            gated_ref[g, r] = (query_ref[rows, :].astype(jnp.float32) * filtered).astype(jnp.bfloat16)

    turns = []
    for d in range(1, 4):
        to = lax.rem(ch + d, 4)
        came = lax.rem(ch + 4 - d, 4)
        for h in range(2):
            slot = 2 * d + h
            out = remote(
                gated_ref.at[h, to], turned_ref.at[2 * ch + h], turn_send.at[slot], turn_recv.at[slot], ch_id(to)
            )
            out.start()
            back = remote(
                gated_ref.at[h, to], turned_ref.at[2 * came + h], turn_send.at[slot], turn_recv.at[slot], ch_id(to)
            )
            turns.append((out, back))
    own_turns = [
        pltpu.make_async_copy(gated_ref.at[h, ch], turned_ref.at[2 * ch + h], own_sem.at[h]) for h in range(2)
    ]
    for copy in own_turns:
        copy.start()

    multiply(1, across)
    to_mate[0].wait_recv()

    @pl.loop(0, 8)
    def _(r):
        rows = pl.ds(pl.multiple_of(r * piece, piece), piece)
        partial_ref[across, rows, :] += arrived_halves[0, rows, :]

    to_across = remote(partial_ref.at[across], last_half, last_send.at[0], last_recv.at[0], ch_id(across))
    to_across.start()
    multiply(2, mate)
    to_mate[1].start()

    for copy in own_turns:
        copy.wait()
    for out, back in turns:
        back.wait_recv()

    columns = pl.ds(pl.multiple_of(me * length, 128), length)
    mine = pl.ds(pl.multiple_of(ch * piece, piece), piece)
    joins = []
    for d in range(1, 8):
        to = lax.rem(me + d, 8)
        came = lax.rem(me + 8 - d, 8)
        from_columns = pl.ds(pl.multiple_of(came * length, 128), length)
        out = remote(turned_ref.at[to], joined_ref.at[:, columns], join_send.at[d], join_recv.at[d], ctx_id(to))
        out.start()
        back = remote(
            turned_ref.at[to], joined_ref.at[:, from_columns], join_send.at[d], join_recv.at[d], ctx_id(to)
        )
        joins.append((out, back))
    own_join = pltpu.make_async_copy(turned_ref.at[me], joined_ref.at[:, columns], own_sem.at[3])
    own_join.start()

    remote(
        cot_ref.at[first], cots_ref.at[twin, first], p_send.at[0], g_recv.at[z], ctx_id(twin)
    ).wait_recv()
    for side in (1, -1):

        @pl.when(goes(side))
        def _():
            along_first(z, side).start()

    multiply(3, ch)

    def step(s):
        for side in (1, -1):
            origin = z - side * s

            @pl.when((origin >= 0) & (origin <= 3))
            def _():
                for part in range(2):
                    along(origin, side, part).wait_recv()

                    @pl.when(goes(side))
                    def _():
                        along(origin, side, part).start()

                    to_twin_rest(origin, part).start()

        for side in (1, -1):
            origin = z - side * s

            @pl.when((origin >= 0) & (origin <= 3))
            def _():
                along_first(origin, side).wait_recv()

                @pl.when(goes(side))
                def _():
                    along_first(origin, side).start()

    step(1)
    own_join.wait()
    for out, back in joins:
        back.wait_recv()

    def rows_of(index):
        return rows_ref.at[pl.ds(pl.multiple_of(index * piece, piece), piece)]

    wide_across = remote(joined_ref, rows_of(ch), wide_send.at[0], wide_recv.at[0], ch_id(across))
    wide_mate = remote(joined_ref, rows_of(ch), wide_send.at[1], wide_recv.at[1], ch_id(mate))
    wide_own = pltpu.make_async_copy(joined_ref, rows_of(ch), own_sem.at[4])
    wide_across.start()
    wide_mate.start()
    wide_own.start()
    step(2)
    remote(joined_ref, rows_of(across), wide_send.at[0], wide_recv.at[0], ch_id(across)).wait_recv()
    wide_on = remote(rows_of(across), rows_of(across), wide_send.at[2], wide_recv.at[2], ch_id(mate))
    wide_on.start()
    to_mate[1].wait_recv()
    to_across.wait_recv()
    for g in range(2):

        @pl.loop(0, 4)
        def _(r):
            rows = pl.ds(pl.multiple_of(g * group_rows + r * piece, piece), piece)
            output_grad = partial_ref[ch, rows, :] + arrived_halves[1, rows, :] + last_half[rows, :]
            signal_ref[rows, :] = output_grad * query_ref[rows, :].astype(jnp.float32)
            query_grad_ref[rows, :] = (output_grad * filtered_ref[rows, :]).astype(jnp.bfloat16)

        back_part[g] = lax.dot_general(
            out_map_ref[g],
            signal_ref[pl.ds(g * group_rows, group_rows), :],
            (((1,), (1,)), ((), ())),
            precision=lax.Precision.HIGHEST,
            preferred_element_type=jnp.float32,
        )
    back_arrive, back_sent = state_copies(back_part, back_slots, back_send, back_recv, -1)
    step(3)
    back_arrive()
    weigh(returning_ref, behind_ref, back_slots, -1)

    remote(joined_ref, rows_of(mate), wide_send.at[1], wide_recv.at[1], ch_id(mate)).wait_recv()
    remote(rows_of(across), rows_of(far), wide_send.at[2], wide_recv.at[2], ch_id(mate)).wait_recv()
    for origin in range(4):
        for part in range(2):
            block = cots_ref.at[2 * origin + 1 - x, rest_rows[part]]
            remote(block, block, q_send.at[part, origin], q_recv.at[part, origin], ctx_id(twin)).wait_recv()
    to_twin_first().wait_send()
    for origin in range(4):
        for part in range(2):
            to_twin_rest(origin, part).wait_send()
        for side in (1, -1):

            @pl.when(goes(side) & (origin <= z if side > 0 else origin >= z))
            def _():
                for part in range(2):
                    along(origin, side, part).wait_send()
                along_first(origin, side).wait_send()

    for out, back in turns + joins:
        out.wait_send()
    wide_across.wait_send()
    wide_mate.wait_send()
    wide_on.wait_send()
    wide_own.wait()
    cot_copy.wait()
    for copy in to_mate + [to_across]:
        copy.wait_send()
    ahead_sent()
    back_sent()


def move_all(cotangent, weight, part, near, query, ahead, behind, in_map, out_map):
    n_ctx, n_ch = lax.axis_size("ctx"), lax.axis_size("ch")
    rows, length = query.shape
    piece = rows // 2 // n_ch
    width = cotangent.shape[1]
    any_space = pl.BlockSpec(memory_space=pl.ANY)
    vmem = pl.BlockSpec(memory_space=pltpu.VMEM)
    f32, bf16 = jnp.float32, jnp.bfloat16
    dma = pltpu.SemaphoreType.DMA
    cots, gathered, _, _, signal, query_grad, returning = pl.pallas_call(
        functools.partial(move_kernel, CUT),
        out_shape=(
            jax.ShapeDtypeStruct((n_ctx, length, width), bf16),
            jax.ShapeDtypeStruct((rows // 2, n_ctx * length), bf16),
            jax.ShapeDtypeStruct((n_ctx, piece, length), bf16),
            jax.ShapeDtypeStruct((piece, n_ctx * length), bf16),
            jax.ShapeDtypeStruct((rows, length), f32),
            jax.ShapeDtypeStruct((rows, length), bf16),
            jax.ShapeDtypeStruct(part.shape, f32),
        ),
        in_specs=[any_space, any_space] + [vmem] * 8,
        out_specs=[any_space] * 4 + [vmem] * 3,
        scratch_shapes=[
            pltpu.VMEM((n_ctx,) + part.shape, f32),
            pltpu.VMEM((n_ctx,) + part.shape, f32),
            pltpu.VMEM(part.shape, f32),
            pltpu.VMEM(part.shape, f32),
            pltpu.VMEM((rows, length), f32),
            pltpu.VMEM((2, n_ch, piece, length), bf16),
            pltpu.VMEM((n_ch, rows, width), bf16),
            pltpu.VMEM((n_ch, rows, length), f32),
            pltpu.VMEM((2, rows, length), f32),
            pltpu.VMEM((rows, length), f32),
            dma((8,)), dma((8,)), dma((8,)), dma((8,)), dma((4,)), dma((2,)), dma((2,)), dma((1,)), dma((1,)),
            dma((5,)), dma((2, 4)), dma((4,)), dma((2, 4)), dma((2, 2, 4)), dma((2, 4)), dma((1,)), dma((2, 4)),
            dma((8,)), dma((8,)), dma((8,)), dma((8,)), dma((3,)), dma((3,)),
        ],
        compiler_params=pltpu.CompilerParams(
            collective_id=0, has_side_effects=True, vmem_limit_bytes=52 * 1024 * 1024
        ),
        cost_estimate=pl.CostEstimate(flops=0, bytes_accessed=300_000_000, transcendentals=0),
        name="move_all",
    )(cotangent, weight, cotangent, part, near, query, ahead, behind, in_map, out_map)
    return signal, query_grad, returning, gathered, cots.reshape(n_ctx * length, width)


def move_by_collectives(cotangent, weight, part, near, query, ahead, behind, in_map, out_map):
    n_ctx, n_ch = lax.axis_size("ctx"), lax.axis_size("ch")
    groups = part.shape[0]
    rows, length = query.shape
    query_f = query.astype(jnp.float32)
    cots = lax.all_gather(cotangent, "ctx", axis=0, tiled=True)
    partial_grad = lax.dot_general(
        weight, cotangent, (((1,), (1,)), ((), ())), preferred_element_type=jnp.float32
    )
    output_grad = lax.psum_scatter(partial_grad, "ch", scatter_dimension=0, tiled=True)
    entering = jnp.sum(ahead * lax.all_gather(part, "ctx", axis=0), axis=0)
    carried = jnp.einsum("gnc,gnt->gct", entering, in_map, precision=HIGH).reshape(rows, length)
    filtered = near + carried
    gathered = exchange_rows((query_f * filtered).astype(jnp.bfloat16), n_ctx, n_ch)
    signal = output_grad * query_f
    back_part = jnp.einsum("gnl,gcl->gnc", out_map, signal.reshape(groups, rows // groups, length), precision=HIGH)
    returning = jnp.sum(behind * lax.all_gather(back_part, "ctx", axis=0), axis=0)
    query_grad = (output_grad * filtered).astype(jnp.bfloat16)
    return signal, query_grad, returning, gathered, cots


def local(
    query_input, key_input, value_input, decay_rate, residue, doc_ends, out_weight, out_cotangent
):
    rows_here, length = query_input.shape
    n_ctx, n_ch = lax.axis_size("ctx"), lax.axis_size("ch")
    groups = decay_rate.shape[0]
    group_rows = rows_here // groups
    me = lax.axis_index("ctx")
    offsets = jnp.arange(length, dtype=jnp.int32)
    place = offsets.astype(jnp.float32)
    doc_ids = doc_of(doc_ends, me * length + offsets)
    blocks = jnp.arange(n_ctx, dtype=jnp.int32)
    last_ids = doc_of(doc_ends, (blocks + 1) * length - 1)
    previous = jnp.where(me > 0, jnp.sum((doc_ends <= me * length - 1).astype(jnp.int32)), -1)
    last = doc_ids[-1]

    alive_mask = (doc_ids == previous).astype(jnp.float32)
    tail_mask = (doc_ids == last).astype(jnp.float32)
    rate = decay_rate[:, :, None]
    carry_in_map = residue[:, :, None] * jnp.exp(-rate * (place + 1.0)) * alive_mask
    carry_out_map = jnp.exp(-rate * (length - 1.0 - place)) * tail_mask
    back_out_map = jnp.exp(-rate * place) * alive_mask
    back_in_map = residue[:, :, None] * jnp.exp(-rate * (length - place)) * tail_mask
    steps_ahead = me - 1 - blocks
    joined_ahead = (steps_ahead >= 0) & (last_ids == previous)
    ahead_weight = jnp.where(
        joined_ahead[:, None, None],
        jnp.exp(-decay_rate[None] * (length * jnp.maximum(steps_ahead, 0)).astype(jnp.float32)[:, None, None]),
        0.0,
    )
    steps_back = blocks - 1 - me
    before_ids = jnp.concatenate([jnp.full((1,), -1, jnp.int32), last_ids[:-1]])
    joined_back = (steps_back >= 0) & (before_ids == last)
    back_weight = jnp.where(
        joined_back[:, None, None],
        jnp.exp(-decay_rate[None] * (length * jnp.maximum(steps_back, 0)).astype(jnp.float32)[:, None, None]),
        0.0,
    )

    key_f = key_input.astype(jnp.float32)
    value_f = value_input.astype(jnp.float32)
    mixed = (key_f * value_f).reshape(groups, group_rows, length)
    forward_part = jnp.einsum("gnl,gcl->gnc", carry_out_map, mixed, precision=HIGH)
    kernel = local_kernel(decay_rate, residue, doc_ids, length)
    near = jnp.einsum("gcs,gts->gct", mixed, kernel, precision=HIGH).reshape(rows_here, length)
    wide = (n_ctx,) + forward_part.shape
    on_kernel = (n_ctx, n_ch, groups) == (8, 4, 2) and rows_here == 1024 and length == 512
    move = move_all if on_kernel else move_by_collectives
    signal, query_grad, returning, gated_rows, cotangent_all = move(
        out_cotangent,
        out_weight,
        forward_part,
        near,
        query_input,
        jnp.broadcast_to(ahead_weight[..., None], wide),
        jnp.broadcast_to(back_weight[..., None], wide),
        carry_in_map,
        back_out_map,
    )
    signal = signal.reshape(groups, group_rows, length)
    spread = jnp.einsum("gct,gts->gcs", signal, kernel, precision=HIGH)
    spread = spread + jnp.einsum("gnc,gns->gcs", returning, back_in_map, precision=HIGH)
    spread = spread.reshape(rows_here, length)
    key_grad = (spread * value_f).astype(jnp.bfloat16)
    value_grad = (spread * key_f).astype(jnp.bfloat16)

    norm_factor = 1.0 / math.sqrt(length * n_ctx)
    weight_grad = jnp.dot(gated_rows, cotangent_all, preferred_element_type=jnp.float32) * norm_factor
    return (query_grad, key_grad, value_grad, weight_grad)


def solution(mesh):
    return jax.shard_map(
        local,
        mesh=mesh,
        in_specs=(
            P("ch", "ctx"),
            P("ch", "ctx"),
            P("ch", "ctx"),
            P("ch", None),
            P("ch", None),
            P(),
            P(None, "ch"),
            P("ctx", "ch"),
        ),
        out_specs=(P("ch", "ctx"), P("ch", "ctx"), P("ch", "ctx"), P("ctx", "ch")),
        check_vma=False,
    )
```

```python
import functools
import math

import jax
import jax.numpy as jnp
from jax import lax
from jax.experimental import pallas as pl
from jax.experimental.pallas import tpu as pltpu
from jax.sharding import PartitionSpec as P

MESH = pl.DeviceIdType.MESH
HIGH = lax.Precision.HIGH
TILE = 128
CUT = 16
PARTS = 4


def doc_of(doc_ends, positions):
    return jnp.sum((doc_ends[None, :] <= positions[:, None]).astype(jnp.int32), axis=1)


def local_kernel(decay_rate, residue, doc_ids, length):
    groups = decay_rate.shape[0]
    place = jnp.arange(length, dtype=jnp.float32)
    narrow = jnp.arange(TILE, dtype=jnp.float32)
    half = 0.5 * TILE
    rising = jnp.exp(-decay_rate[:, None, :] * (place - half)[None, :, None]) * residue[:, None, :]
    falling = jnp.exp(decay_rate[:, None, :] * (narrow - half)[None, :, None])
    strip = jnp.einsum("gtn,gsn->gts", rising, falling, precision=lax.Precision.HIGHEST)
    columns = []
    for start in range(0, length, TILE):
        top = jnp.zeros((groups, start, TILE), jnp.float32)
        columns.append(jnp.concatenate([top, strip[:, : length - start]], axis=1))
    kernel = jnp.concatenate(columns, axis=2)
    offsets = jnp.arange(length, dtype=jnp.int32)
    causal = (offsets[:, None] >= offsets[None, :]) & (doc_ids[:, None] == doc_ids[None, :])
    return jnp.where(causal[None], kernel, 0.0)


def exchange_rows(gated, n_ctx, n_ch):
    rows, length = gated.shape
    mine = rows * n_ch // n_ctx
    pieces = gated.reshape(n_ctx // n_ch, n_ch, mine // n_ch, length)
    pieces = lax.all_to_all(pieces, "ch", split_axis=1, concat_axis=0, tiled=True)
    pieces = pieces.reshape(n_ctx, mine // n_ch, length)
    pieces = lax.all_to_all(pieces, "ctx", split_axis=0, concat_axis=0, tiled=True)
    pieces = pieces.transpose(1, 0, 2).reshape(mine // n_ch, n_ctx * length)
    return lax.all_gather(pieces, "ch", axis=0, tiled=True)


def ctx_id(index):
    return (index, lax.axis_index("ch"))


def ch_id(index):
    return (lax.axis_index("ctx"), index)


def remote(src, dst, send, recv, device):
    return pltpu.make_async_remote_copy(
        src_ref=src, dst_ref=dst, send_sem=send, recv_sem=recv, device_id=device, device_id_type=MESH
    )


def greet(devices):
    barrier = pltpu.get_barrier_semaphore()
    for device in devices:
        pl.semaphore_signal(barrier, inc=1, device_id=device, device_id_type=MESH)
    pl.semaphore_wait(barrier, len(devices))


def inside(index):
    return (index >= 0) & (index < 8)


def state_copies(part, slots, send, recv, sign):
    me = lax.axis_index("ctx")
    for d in range(1, 8):
        to = me + sign * d

        @pl.when(inside(to))
        def _():
            remote(part, slots.at[me], send.at[d], recv.at[d], ctx_id(to)).start()

    def arrive():
        for d in range(1, 8):
            came = me - sign * d

            @pl.when(inside(came))
            def _():
                remote(part, slots.at[came], send.at[d], recv.at[d], ctx_id(came)).wait_recv()

    def sent():
        for d in range(1, 8):
            to = me + sign * d

            @pl.when(inside(to))
            def _():
                remote(part, slots.at[me], send.at[d], recv.at[d], ctx_id(to)).wait_send()

    return arrive, sent


def weigh(total, weight, slots, sign):
    me = lax.axis_index("ctx")
    total[...] = jnp.zeros_like(total)
    for k in range(8):

        @pl.when(k < me if sign > 0 else k > me)
        def _():
            total[...] += weight[k] * slots[k]


def move_kernel(
    cut, cot_ref, weight_ref, cot_near, part_ref, near_ref, query_ref, ahead_ref, behind_ref, in_map_ref, out_map_ref,
    cots_ref, rows_ref, turned_ref, joined_ref, signal_ref, query_grad_ref, returning_ref,
    ahead_slots, back_slots, back_part, entering, filtered_ref, gated_ref, weights, partial_ref, arrived_halves, last_half,
    ahead_send, ahead_recv, back_send, back_recv, half_sem, half_send, half_recv, last_send, last_recv,
    own_sem, f_recv, g_recv, q_recv, f_send, g_send, p_send, q_send,
    turn_send, turn_recv, join_send, join_recv, wide_send, wide_recv,
):
    me, ch = lax.axis_index("ctx"), lax.axis_index("ch")
    z, x = me // 2, me % 2
    twin = me + 1 - 2 * x
    y, core = ch // 2, ch % 2
    across = (1 - y) * 2 + core
    mate = y * 2 + 1 - core
    far = (1 - y) * 2 + 1 - core
    length = cot_ref.shape[0]
    piece = turned_ref.shape[1]
    group_rows = 4 * piece
    greet(
        [ctx_id(lax.rem(me + d, 8)) for d in range(1, 8)]
        + [ch_id(lax.rem(ch + d, 4)) for d in range(1, 4)]
    )
    first = pl.ds(0, cut)
    ahead_arrive, ahead_sent = state_copies(part_ref, ahead_slots, ahead_send, ahead_recv, 1)

    to_mate = [
        remote(partial_ref.at[index], arrived_halves.at[k], half_send.at[k], half_recv.at[k], ch_id(mate))
        for k, index in ((0, far), (1, mate))
    ]
    rows_here = last_half.shape[0]
    load_weights = [
        pltpu.make_async_copy(
            weight_ref.at[pl.ds(pl.multiple_of(index * rows_here, rows_here), rows_here)],
            weights.at[k],
            half_sem.at[k],
        )
        for k, index in enumerate((far, across, mate, ch))
    ]

    def multiply(k, index):
        load_weights[k].wait()

        @pl.loop(0, 4)
        def _(r):
            rows = pl.ds(pl.multiple_of(r * 2 * piece, piece), 2 * piece)
            partial_ref[index, rows, :] = lax.dot_general(
                weights[k, rows, :], cot_near[...], (((1,), (1,)), ((), ())), preferred_element_type=jnp.float32
            )

    cot_copy = pltpu.make_async_copy(cot_ref, cots_ref.at[me], own_sem.at[2])

    def to_twin_first():
        return remote(cot_ref.at[first], cots_ref.at[me, first], p_send.at[0], g_recv.at[z], ctx_id(twin))

    share = length // PARTS
    along_rows = [pl.ds(part * share, share) for part in range(PARTS)]
    rest_rows = [pl.ds(cut, share - cut)] + along_rows[1:]

    def to_twin_rest(origin, part, src=None):
        rows = rest_rows[part]
        to = cots_ref.at[2 * origin + x, rows]
        src = to if src is None else src.at[rows]
        return remote(src, to, q_send.at[part, origin], q_recv.at[part, origin], ctx_id(twin))

    def along(origin, side, part, src=None):
        rows = along_rows[part]
        to = cots_ref.at[2 * origin + x, rows]
        src = to if src is None else src.at[rows]
        way = (side + 1) // 2
        return remote(src, to, f_send.at[way, part, origin], f_recv.at[part, origin], ctx_id(me + 2 * side))

    def along_first(origin, side):
        slot = 2 * origin + 1 - x
        to = me + 2 * side
        part = cots_ref.at[slot, first]
        return remote(part, part, g_send.at[(side + 1) // 2, origin], g_recv.at[origin], ctx_id(to))

    def goes(side):
        return z < 3 if side > 0 else z > 0

    to_twin_first().start()
    for side in (1, -1):

        @pl.when(goes(side))
        def _():
            for part in range(PARTS):
                along(z, side, part, cot_ref).start()

    for part in range(PARTS):
        to_twin_rest(z, part, cot_ref).start()
    for copy in load_weights + [cot_copy]:
        copy.start()
    multiply(0, far)
    to_mate[0].start()

    ahead_arrive()
    weigh(entering, ahead_ref, ahead_slots, 1)
    for g in range(2):
        carried = entering[g].T

        for r in range(4):
            rows = pl.ds(g * group_rows + r * piece, piece)
            filtered = near_ref[rows, :] + jnp.dot(
                carried[r * piece : (r + 1) * piece],
                in_map_ref[g],
                precision=lax.Precision.HIGHEST,
                preferred_element_type=jnp.float32,
            )
            filtered_ref[rows, :] = filtered
            gated_ref[g, r] = (query_ref[rows, :].astype(jnp.float32) * filtered).astype(jnp.bfloat16)

    turns = []
    for d in range(1, 4):
        to = lax.rem(ch + d, 4)
        came = lax.rem(ch + 4 - d, 4)
        for h in range(2):
            slot = 2 * d + h
            out = remote(
                gated_ref.at[h, to], turned_ref.at[2 * ch + h], turn_send.at[slot], turn_recv.at[slot], ch_id(to)
            )
            out.start()
            back = remote(
                gated_ref.at[h, to], turned_ref.at[2 * came + h], turn_send.at[slot], turn_recv.at[slot], ch_id(to)
            )
            turns.append((out, back))
    own_turns = [
        pltpu.make_async_copy(gated_ref.at[h, ch], turned_ref.at[2 * ch + h], own_sem.at[h]) for h in range(2)
    ]
    for copy in own_turns:
        copy.start()

    multiply(1, across)
    to_mate[0].wait_recv()

    @pl.loop(0, 8)
    def _(r):
        rows = pl.ds(pl.multiple_of(r * piece, piece), piece)
        partial_ref[across, rows, :] += arrived_halves[0, rows, :]

    to_across = remote(partial_ref.at[across], last_half, last_send.at[0], last_recv.at[0], ch_id(across))
    to_across.start()
    multiply(2, mate)
    to_mate[1].start()

    for copy in own_turns:
        copy.wait()
    for out, back in turns:
        back.wait_recv()

    columns = pl.ds(pl.multiple_of(me * length, 128), length)
    mine = pl.ds(pl.multiple_of(ch * piece, piece), piece)
    joins = []
    for d in range(1, 8):
        to = lax.rem(me + d, 8)
        came = lax.rem(me + 8 - d, 8)
        from_columns = pl.ds(pl.multiple_of(came * length, 128), length)
        out = remote(turned_ref.at[to], joined_ref.at[:, columns], join_send.at[d], join_recv.at[d], ctx_id(to))
        out.start()
        back = remote(
            turned_ref.at[to], joined_ref.at[:, from_columns], join_send.at[d], join_recv.at[d], ctx_id(to)
        )
        joins.append((out, back))
    own_join = pltpu.make_async_copy(turned_ref.at[me], joined_ref.at[:, columns], own_sem.at[3])
    own_join.start()

    remote(
        cot_ref.at[first], cots_ref.at[twin, first], p_send.at[0], g_recv.at[z], ctx_id(twin)
    ).wait_recv()
    for side in (1, -1):

        @pl.when(goes(side))
        def _():
            along_first(z, side).start()

    multiply(3, ch)

    def step(s):
        for side in (1, -1):
            origin = z - side * s

            @pl.when((origin >= 0) & (origin <= 3))
            def _():
                for part in range(PARTS):
                    along(origin, side, part).wait_recv()

                    @pl.when(goes(side))
                    def _():
                        along(origin, side, part).start()

                    to_twin_rest(origin, part).start()

        for side in (1, -1):
            origin = z - side * s

            @pl.when((origin >= 0) & (origin <= 3))
            def _():
                along_first(origin, side).wait_recv()

                @pl.when(goes(side))
                def _():
                    along_first(origin, side).start()

    step(1)
    own_join.wait()
    for out, back in joins:
        back.wait_recv()

    def rows_of(index):
        return rows_ref.at[pl.ds(pl.multiple_of(index * piece, piece), piece)]

    wide_across = remote(joined_ref, rows_of(ch), wide_send.at[0], wide_recv.at[0], ch_id(across))
    wide_mate = remote(joined_ref, rows_of(ch), wide_send.at[1], wide_recv.at[1], ch_id(mate))
    wide_own = pltpu.make_async_copy(joined_ref, rows_of(ch), own_sem.at[4])
    wide_across.start()
    wide_mate.start()
    wide_own.start()
    step(2)
    remote(joined_ref, rows_of(across), wide_send.at[0], wide_recv.at[0], ch_id(across)).wait_recv()
    wide_on = remote(rows_of(across), rows_of(across), wide_send.at[2], wide_recv.at[2], ch_id(mate))
    wide_on.start()
    to_mate[1].wait_recv()
    to_across.wait_recv()
    for g in range(2):

        @pl.loop(0, 4)
        def _(r):
            rows = pl.ds(pl.multiple_of(g * group_rows + r * piece, piece), piece)
            output_grad = partial_ref[ch, rows, :] + arrived_halves[1, rows, :] + last_half[rows, :]
            signal_ref[rows, :] = output_grad * query_ref[rows, :].astype(jnp.float32)
            query_grad_ref[rows, :] = (output_grad * filtered_ref[rows, :]).astype(jnp.bfloat16)

        back_part[g] = lax.dot_general(
            out_map_ref[g],
            signal_ref[pl.ds(g * group_rows, group_rows), :],
            (((1,), (1,)), ((), ())),
            precision=lax.Precision.HIGHEST,
            preferred_element_type=jnp.float32,
        )
    back_arrive, back_sent = state_copies(back_part, back_slots, back_send, back_recv, -1)
    step(3)
    back_arrive()
    weigh(returning_ref, behind_ref, back_slots, -1)

    remote(joined_ref, rows_of(mate), wide_send.at[1], wide_recv.at[1], ch_id(mate)).wait_recv()
    remote(rows_of(across), rows_of(far), wide_send.at[2], wide_recv.at[2], ch_id(mate)).wait_recv()
    for origin in range(4):
        for part in range(PARTS):
            block = cots_ref.at[2 * origin + 1 - x, rest_rows[part]]
            remote(block, block, q_send.at[part, origin], q_recv.at[part, origin], ctx_id(twin)).wait_recv()
    to_twin_first().wait_send()
    for origin in range(4):
        for part in range(PARTS):
            to_twin_rest(origin, part).wait_send()
        for side in (1, -1):

            @pl.when(goes(side) & (origin <= z if side > 0 else origin >= z))
            def _():
                for part in range(PARTS):
                    along(origin, side, part).wait_send()
                along_first(origin, side).wait_send()

    for out, back in turns + joins:
        out.wait_send()
    wide_across.wait_send()
    wide_mate.wait_send()
    wide_on.wait_send()
    wide_own.wait()
    cot_copy.wait()
    for copy in to_mate + [to_across]:
        copy.wait_send()
    ahead_sent()
    back_sent()


def move_all(cotangent, weight, part, near, query, ahead, behind, in_map, out_map):
    n_ctx, n_ch = lax.axis_size("ctx"), lax.axis_size("ch")
    rows, length = query.shape
    piece = rows // 2 // n_ch
    width = cotangent.shape[1]
    any_space = pl.BlockSpec(memory_space=pl.ANY)
    vmem = pl.BlockSpec(memory_space=pltpu.VMEM)
    f32, bf16 = jnp.float32, jnp.bfloat16
    dma = pltpu.SemaphoreType.DMA
    cots, gathered, _, _, signal, query_grad, returning = pl.pallas_call(
        functools.partial(move_kernel, CUT),
        out_shape=(
            jax.ShapeDtypeStruct((n_ctx, length, width), bf16),
            jax.ShapeDtypeStruct((rows // 2, n_ctx * length), bf16),
            jax.ShapeDtypeStruct((n_ctx, piece, length), bf16),
            jax.ShapeDtypeStruct((piece, n_ctx * length), bf16),
            jax.ShapeDtypeStruct((rows, length), f32),
            jax.ShapeDtypeStruct((rows, length), bf16),
            jax.ShapeDtypeStruct(part.shape, f32),
        ),
        in_specs=[any_space, any_space] + [vmem] * 8,
        out_specs=[any_space] * 4 + [vmem] * 3,
        scratch_shapes=[
            pltpu.VMEM((n_ctx,) + part.shape, f32),
            pltpu.VMEM((n_ctx,) + part.shape, f32),
            pltpu.VMEM(part.shape, f32),
            pltpu.VMEM(part.shape, f32),
            pltpu.VMEM((rows, length), f32),
            pltpu.VMEM((2, n_ch, piece, length), bf16),
            pltpu.VMEM((n_ch, rows, width), bf16),
            pltpu.VMEM((n_ch, rows, length), f32),
            pltpu.VMEM((2, rows, length), f32),
            pltpu.VMEM((rows, length), f32),
            dma((8,)), dma((8,)), dma((8,)), dma((8,)), dma((4,)), dma((2,)), dma((2,)), dma((1,)), dma((1,)),
            dma((5,)), dma((PARTS, 4)), dma((4,)), dma((PARTS, 4)), dma((2, PARTS, 4)), dma((2, 4)), dma((1,)),
            dma((PARTS, 4)),
            dma((8,)), dma((8,)), dma((8,)), dma((8,)), dma((3,)), dma((3,)),
        ],
        compiler_params=pltpu.CompilerParams(
            collective_id=0, has_side_effects=True, vmem_limit_bytes=52 * 1024 * 1024
        ),
        cost_estimate=pl.CostEstimate(flops=0, bytes_accessed=300_000_000, transcendentals=0),
        name="move_all",
    )(cotangent, weight, cotangent, part, near, query, ahead, behind, in_map, out_map)
    return signal, query_grad, returning, gathered, cots.reshape(n_ctx * length, width)


def move_by_collectives(cotangent, weight, part, near, query, ahead, behind, in_map, out_map):
    n_ctx, n_ch = lax.axis_size("ctx"), lax.axis_size("ch")
    groups = part.shape[0]
    rows, length = query.shape
    query_f = query.astype(jnp.float32)
    cots = lax.all_gather(cotangent, "ctx", axis=0, tiled=True)
    partial_grad = lax.dot_general(
        weight, cotangent, (((1,), (1,)), ((), ())), preferred_element_type=jnp.float32
    )
    output_grad = lax.psum_scatter(partial_grad, "ch", scatter_dimension=0, tiled=True)
    entering = jnp.sum(ahead * lax.all_gather(part, "ctx", axis=0), axis=0)
    carried = jnp.einsum("gnc,gnt->gct", entering, in_map, precision=HIGH).reshape(rows, length)
    filtered = near + carried
    gathered = exchange_rows((query_f * filtered).astype(jnp.bfloat16), n_ctx, n_ch)
    signal = output_grad * query_f
    back_part = jnp.einsum("gnl,gcl->gnc", out_map, signal.reshape(groups, rows // groups, length), precision=HIGH)
    returning = jnp.sum(behind * lax.all_gather(back_part, "ctx", axis=0), axis=0)
    query_grad = (output_grad * filtered).astype(jnp.bfloat16)
    return signal, query_grad, returning, gathered, cots


def local(
    query_input, key_input, value_input, decay_rate, residue, doc_ends, out_weight, out_cotangent
):
    rows_here, length = query_input.shape
    n_ctx, n_ch = lax.axis_size("ctx"), lax.axis_size("ch")
    groups = decay_rate.shape[0]
    group_rows = rows_here // groups
    me = lax.axis_index("ctx")
    offsets = jnp.arange(length, dtype=jnp.int32)
    place = offsets.astype(jnp.float32)
    doc_ids = doc_of(doc_ends, me * length + offsets)
    blocks = jnp.arange(n_ctx, dtype=jnp.int32)
    last_ids = doc_of(doc_ends, (blocks + 1) * length - 1)
    previous = jnp.where(me > 0, jnp.sum((doc_ends <= me * length - 1).astype(jnp.int32)), -1)
    last = doc_ids[-1]

    alive_mask = (doc_ids == previous).astype(jnp.float32)
    tail_mask = (doc_ids == last).astype(jnp.float32)
    rate = decay_rate[:, :, None]
    carry_in_map = residue[:, :, None] * jnp.exp(-rate * (place + 1.0)) * alive_mask
    carry_out_map = jnp.exp(-rate * (length - 1.0 - place)) * tail_mask
    back_out_map = jnp.exp(-rate * place) * alive_mask
    back_in_map = residue[:, :, None] * jnp.exp(-rate * (length - place)) * tail_mask
    steps_ahead = me - 1 - blocks
    joined_ahead = (steps_ahead >= 0) & (last_ids == previous)
    ahead_weight = jnp.where(
        joined_ahead[:, None, None],
        jnp.exp(-decay_rate[None] * (length * jnp.maximum(steps_ahead, 0)).astype(jnp.float32)[:, None, None]),
        0.0,
    )
    steps_back = blocks - 1 - me
    before_ids = jnp.concatenate([jnp.full((1,), -1, jnp.int32), last_ids[:-1]])
    joined_back = (steps_back >= 0) & (before_ids == last)
    back_weight = jnp.where(
        joined_back[:, None, None],
        jnp.exp(-decay_rate[None] * (length * jnp.maximum(steps_back, 0)).astype(jnp.float32)[:, None, None]),
        0.0,
    )

    key_f = key_input.astype(jnp.float32)
    value_f = value_input.astype(jnp.float32)
    mixed = (key_f * value_f).reshape(groups, group_rows, length)
    forward_part = jnp.einsum("gnl,gcl->gnc", carry_out_map, mixed, precision=HIGH)
    kernel = local_kernel(decay_rate, residue, doc_ids, length)
    near = jnp.einsum("gcs,gts->gct", mixed, kernel, precision=HIGH).reshape(rows_here, length)
    wide = (n_ctx,) + forward_part.shape
    on_kernel = (n_ctx, n_ch, groups) == (8, 4, 2) and rows_here == 1024 and length == 512
    move = move_all if on_kernel else move_by_collectives
    signal, query_grad, returning, gated_rows, cotangent_all = move(
        out_cotangent,
        out_weight,
        forward_part,
        near,
        query_input,
        jnp.broadcast_to(ahead_weight[..., None], wide),
        jnp.broadcast_to(back_weight[..., None], wide),
        carry_in_map,
        back_out_map,
    )
    signal = signal.reshape(groups, group_rows, length)
    spread = jnp.einsum("gct,gts->gcs", signal, kernel, precision=HIGH)
    spread = spread + jnp.einsum("gnc,gns->gcs", returning, back_in_map, precision=HIGH)
    spread = spread.reshape(rows_here, length)
    key_grad = (spread * value_f).astype(jnp.bfloat16)
    value_grad = (spread * key_f).astype(jnp.bfloat16)

    norm_factor = 1.0 / math.sqrt(length * n_ctx)
    weight_grad = jnp.dot(gated_rows, cotangent_all, preferred_element_type=jnp.float32) * norm_factor
    return (query_grad, key_grad, value_grad, weight_grad)


def solution(mesh):
    return jax.shard_map(
        local,
        mesh=mesh,
        in_specs=(
            P("ch", "ctx"),
            P("ch", "ctx"),
            P("ch", "ctx"),
            P("ch", None),
            P("ch", None),
            P(),
            P(None, "ch"),
            P("ctx", "ch"),
        ),
        out_specs=(P("ch", "ctx"), P("ch", "ctx"), P("ch", "ctx"), P("ctx", "ch")),
        check_vma=False,
    )
```
